32 devices in a mesh: seq: 8 (over z, x), head: 4 (over y, core).
Axes of the slice: x: 2, y: 2, z: 4, core: 2. Of those that a mesh axis runs over, the one named last changes fastest.
Arguments:
- hidden: bfloat16 [1, 2048, 1024], P(None, 'seq'), may hold values from -6 to 6
- cotangent: bfloat16 [1, 2048, 1024], P(None, 'seq'), may hold values from -6 to 6
- pre_gain: float32 [1024], replicated, may hold values from 0.5 to 1.5
- w_zx: bfloat16 [1024, 2, 2048], P(None, None, 'head'), may hold values from -0.1875 to 0.1875
- w_bc: bfloat16 [1024, 256], replicated, may hold values from -0.1875 to 0.1875
- w_dt: bfloat16 [1024, 32], P(None, 'head'), may hold values from -0.1875 to 0.1875
- conv_x_w: float32 [4, 2048], P(None, 'head'), may hold values from -0.5 to 0.5
- conv_x_b: float32 [2048], P('head'), may hold values from -0.5 to 0.5
- conv_bc_w: float32 [4, 256], replicated, may hold values from -0.5 to 0.5
- conv_bc_b: float32 [256], replicated, may hold values from -0.5 to 0.5
- dt_bias: float32 [32], P('head'), may hold values from -4.5 to -2.5
- a_log: float32 [32], P('head'), as said below
- d_skip: float32 [32], P('head'), may hold values from 0.5 to 1.5
- gate_gain: float32 [2048], P('head'), may hold values from 0.5 to 1.5
- w_out: bfloat16 [2048, 1024], P('head'), may hold values from -0.125 to 0.125
Outputs:
- output: bfloat16 [1, 2048, 1024], P(None, 'seq')
- grad_hidden: float32 [1, 2048, 1024], P(None, 'seq')
- grad_pre_gain: float32 [1024], replicated
- grad_w_zx: float32 [1024, 2, 2048], P('seq', None, 'head')
- grad_w_bc: float32 [1024, 256], P('seq')
- grad_w_dt: float32 [1024, 32], P('seq', 'head')
- grad_conv_x_w: float32 [4, 2048], P(None, 'head')
- grad_conv_x_b: float32 [2048], P('head')
- grad_conv_bc_w: float32 [4, 256], replicated
- grad_conv_bc_b: float32 [256], replicated
- grad_dt_bias: float32 [32], P('head')
- grad_a_log: float32 [32], P('head')
- grad_d_skip: float32 [32], P('head')
- grad_gate_gain: float32 [2048], P('head')
- grad_w_out: float32 [2048, 1024], P('head', 'seq')
The draws below stay inside these ranges and needn't reach their ends.
Inputs may be any that keep to these rules, and one draw needn't show every extreme that they name: Each head's decay rate exp(a_log) lies between 2.4 / 2048 and 2.
All inputs are finite; a program needn't handle non-finite values.
Results may differ from the reference program's by a relative error of at most 0.003.
The reference program's roundings to bfloat16 on the way count: a program that leaves them out, or rounds other values in their place, can miss the bound.
Values may be sent and summed in bfloat16 or wider, within the bound.
A program may use at most 128 MiB of HBM per device.

```python
import math
import jax
import jax.numpy as jnp
from jax import lax

D = 1024
DI = 2048
H = 32
P_SIZE = 64
NS = 128
KW = 4
BLOCK = 256
SEQS = 1
LENGTH = 2048


def draw_a_log(key, part):
    first, second, third = jax.random.split(key, 3)
    chooser = jax.random.uniform(first, (H,))
    share = 0.5
    fast_rate = jnp.exp(jax.random.uniform(second, (H,), minval=math.log(0.5), maxval=math.log(2.0)))
    slow_rate = 8.0 / LENGTH * jnp.exp(jax.random.uniform(third, (H,), minval=math.log(0.3), maxval=math.log(1.5)))
    return jnp.log(jnp.where(chooser < share, fast_rate, slow_rate)).astype(jnp.float32)


def steps_of(stream_key, dims, shards, low, high):
    factor_of, own = 1.0, jax.random.fold_in(stream_key, 6)
    for dim, parts in shards:
        heights = jnp.exp(jax.random.uniform(jax.random.fold_in(own, dim), (parts,), jnp.float32, low / len(shards), high / len(shards)))
        factor_of = factor_of * jnp.repeat(heights, dims[dim] // parts).reshape([-1 if axis == dim else 1 for axis in range(len(dims))])
    return factor_of


def gaussian(key, shape, scale, bound, cuts=(), dtype=jnp.bfloat16):
    level = steps_of(key, shape, cuts, -0.22, 0.18) if cuts else 1.0
    result = jax.random.normal(key, shape, jnp.float32) * scale * level
    return jnp.minimum(jnp.maximum(result, -bound), bound).astype(dtype)


def setup_inputs(seed: int = 0) -> dict:
    arg_keys = jax.random.split(jax.random.key(seed), 16)
    hidden = gaussian(arg_keys[0], (SEQS, LENGTH, D), 1.0, 6.0, ((1, 8),))
    cotangent = gaussian(arg_keys[1], (SEQS, LENGTH, D), 1.0, 6.0, ((1, 8),))
    pre_gain = jnp.clip(1.0 + 0.1 * jax.random.normal(arg_keys[2], (D,), jnp.float32), 0.5, 1.5)
    w_zx = gaussian(arg_keys[3], (D, 2, DI), D ** -0.5, 0.1875, ((2, 4),))
    w_bc = gaussian(arg_keys[4], (D, 2 * NS), D ** -0.5, 0.1875)
    w_dt = gaussian(arg_keys[5], (D, H), D ** -0.5, 0.1875, ((1, 4),))
    conv_x_w = jnp.clip(jax.random.uniform(arg_keys[6], (KW, DI), jnp.float32, -0.5, 0.5) * steps_of(arg_keys[6], (KW, DI), ((1, 4),), -0.4, 0.0), -0.5, 0.5)
    conv_x_b = jnp.clip(jax.random.uniform(arg_keys[7], (DI,), jnp.float32, -0.5, 0.5) * steps_of(arg_keys[7], (DI,), ((0, 4),), -0.4, 0.0), -0.5, 0.5)
    conv_bc_w = jnp.clip(jax.random.uniform(arg_keys[8], (KW, 2 * NS), jnp.float32, -0.5, 0.5), -0.5, 0.5)
    conv_bc_b = jnp.clip(jax.random.uniform(arg_keys[9], (2 * NS,), jnp.float32, -0.5, 0.5), -0.5, 0.5)
    dt_bias = jnp.clip(-4.5 + 2.0 * jax.random.uniform(arg_keys[10], (H,), jnp.float32) ** steps_of(arg_keys[10], (H,), ((0, 4),), -0.2, 0.2), -4.5, -2.5)
    a_log = draw_a_log(jax.random.fold_in(arg_keys[15], 71), 0)
    d_skip = jnp.clip(0.5 + 1.0 * jax.random.uniform(arg_keys[12], (H,), jnp.float32) ** steps_of(arg_keys[12], (H,), ((0, 4),), -0.2, 0.2), 0.5, 1.5)
    gate_gain = jnp.clip(1.0 + 0.1 * jax.random.normal(arg_keys[13], (DI,), jnp.float32), 0.5, 1.5)
    w_out = gaussian(arg_keys[14], (DI, D), DI ** -0.5, 0.125, ((0, 4),))
    return dict(hidden=hidden, cotangent=cotangent, pre_gain=pre_gain, w_zx=w_zx, w_bc=w_bc, w_dt=w_dt, conv_x_w=conv_x_w, conv_x_b=conv_x_b, conv_bc_w=conv_bc_w, conv_bc_b=conv_bc_b, dt_bias=dt_bias, a_log=a_log, d_skip=d_skip, gate_gain=gate_gain, w_out=w_out)


@jax.custom_vjp
def low(v):
    return lax.optimization_barrier(v.astype(jnp.bfloat16)).astype(jnp.float32)

@jax.custom_vjp
def low_back(v):
    return v

def low_keep(v):
    return (low(v), None)

def low_pass(kept, grad):
    return (grad,)

def back_keep(v):
    return (v, None)

def back_low(kept, grad):
    return (low(grad),)
low.defvjp(low_keep, low_pass)
low_back.defvjp(back_keep, back_low)
EPSILON = 1e-05
HIGHEST = lax.Precision.HIGHEST

def causal_conv(values, weight, offset_b):
    length = values.shape[0]
    padded = jnp.pad(values, ((KW - 1, 0), (0, 0)))
    summed = offset_b + weight[0] * padded[0:length]
    for offset in range(1, KW):
        summed = summed + weight[offset] * padded[offset:offset + length]
    return summed

def block_step(carried, inputs):
    x_heads, b_mat, c_mat, deltas, log_decay = inputs
    cumulative = jnp.cumsum(log_decay, axis=0)
    scores = jnp.dot(c_mat, b_mat.T, precision=HIGHEST)
    row_ids = lax.broadcasted_iota(jnp.int32, (BLOCK, BLOCK), 0)
    column_ids = lax.broadcasted_iota(jnp.int32, (BLOCK, BLOCK), 1)
    causal = (row_ids >= column_ids)[:, :, None]
    spread = cumulative[:, None, :] - cumulative[None, :, :]
    decays = jnp.where(causal, jnp.exp(jnp.where(causal, spread, 0.0)), 0.0)
    weights = scores[:, :, None] * decays * deltas[None, :, :]
    inside = jnp.einsum('tsh,shp->thp', weights, x_heads, precision=HIGHEST)
    outside = jnp.exp(cumulative)[:, :, None] * jnp.einsum('tn,hpn->thp', c_mat, carried, precision=HIGHEST)
    tail_w = jnp.exp(cumulative[-1][None, :] - cumulative) * deltas
    local_state = jnp.einsum('shp,sn->hpn', tail_w[:, :, None] * x_heads, b_mat, precision=HIGHEST)
    carried = jnp.exp(cumulative[-1])[:, None, None] * carried + local_state
    return (carried, inside + outside)

def sequence(residual, params):
    pre_gain, w_zx, w_bc, w_dt, conv_x_w, conv_x_b, conv_bc_w, conv_bc_b, dt_bias, a_log, d_skip, gate_gain, w_out = params
    length = residual.shape[0]
    in_rstd = lax.rsqrt(lax.optimization_barrier(jnp.mean(residual * residual, axis=-1, keepdims=True)) + EPSILON)
    normed_in = low(residual * in_rstd * pre_gain)
    projected = low_back(jnp.einsum('ld,dke->lke', normed_in, w_zx, precision=HIGHEST))
    gating = projected[:, 0]
    conv_in = low(projected[:, 1])
    bc_in = low(low_back(jnp.dot(normed_in, w_bc, precision=HIGHEST)))
    dt_raw = low_back(jnp.dot(normed_in, w_dt, precision=HIGHEST))
    x_heads = low(jax.nn.silu(causal_conv(conv_in, conv_x_w, conv_x_b))).reshape(length, H, P_SIZE)
    bc_post = jax.nn.silu(causal_conv(bc_in, conv_bc_w, conv_bc_b))
    b_mat = low(bc_post[:, :NS])
    c_mat = low(bc_post[:, NS:])
    deltas = jax.nn.softplus(dt_raw + dt_bias)
    log_decay = deltas * -jnp.exp(a_log)
    block_count = length // BLOCK
    inputs = (x_heads.reshape(block_count, BLOCK, H, P_SIZE), b_mat.reshape(block_count, BLOCK, NS), c_mat.reshape(block_count, BLOCK, NS), deltas.reshape(block_count, BLOCK, H), log_decay.reshape(block_count, BLOCK, H))
    initial = jnp.zeros((H, P_SIZE, NS), jnp.float32)
    _, mixed = lax.scan(jax.checkpoint(block_step), initial, inputs)
    ssd_out = mixed.reshape(length, H, P_SIZE) + d_skip[None, :, None] * x_heads
    gated = ssd_out.reshape(length, DI) * jax.nn.silu(gating)
    gate_rstd = lax.rsqrt(lax.optimization_barrier(jnp.mean(gated * gated, axis=-1, keepdims=True)) + EPSILON)
    normed_out = low(gated * gate_rstd * gate_gain)
    return residual + jnp.dot(normed_out, w_out, precision=HIGHEST)

def layer(hidden, params):

    def one_sequence(sequence_in):
        return sequence(sequence_in, params)
    return lax.map(jax.checkpoint(one_sequence), hidden)

def reference(hidden, cotangent, pre_gain, w_zx, w_bc, w_dt, conv_x_w, conv_x_b, conv_bc_w, conv_bc_b, dt_bias, a_log, d_skip, gate_gain, w_out):
    params = tuple((entry.astype(jnp.float32) for entry in (pre_gain, w_zx, w_bc, w_dt, conv_x_w, conv_x_b, conv_bc_w, conv_bc_b, dt_bias, a_log, d_skip, gate_gain, w_out)))
    output, pullback = jax.vjp(layer, hidden.astype(jnp.float32), params)
    grad_hidden, gradients = pullback(cotangent.astype(jnp.float32))
    return (output.astype(jnp.bfloat16), grad_hidden, gradients[0], gradients[1], gradients[2], gradients[3], gradients[4], gradients[5], gradients[6], gradients[7], gradients[8], gradients[9], gradients[10], gradients[11], gradients[12])
```

```python
import functools

import jax
import jax.numpy as jnp
from jax import lax
from jax.experimental import pallas as pl
from jax.experimental.pallas import tpu as pltpu
from jax.sharding import PartitionSpec as P

MESH = pl.DeviceIdType.MESH
VMEM = pltpu.VMEM
DMA = pltpu.SemaphoreType.DMA
IN_VMEM = pl.BlockSpec(memory_space=pltpu.VMEM)
ANYWHERE = pl.BlockSpec(memory_space=pl.ANY)

EPSILON = 1e-05
HALO = 16
LANES = 128
BF16, F32 = jnp.bfloat16, jnp.float32
NN, NT = ((1,), (0,)), ((1,), (1,))


def split(value, parts):
    if value.dtype == BF16:
        return [value]
    terms = []
    for at in range(parts):
        terms.append(value.astype(BF16))
        if at < parts - 1:
            value = value - terms[-1].astype(F32)
    return terms


def mm(left, right, dims, left_parts=1, right_parts=1):
    total = None
    most = max(left_parts, right_parts)
    rights = split(right, right_parts)
    for i, a in enumerate(split(left, left_parts)):
        for k, b in enumerate(rights):
            if i + k < most:
                term = lax.dot_general(a, b, (dims, ((), ())), preferred_element_type=F32)
                total = term if total is None else total + term
    return total


def low(values):
    return values.astype(BF16).astype(F32)


def softplus(values):
    return jnp.maximum(values, 0.0) + jnp.log1p(jnp.exp(-jnp.abs(values)))


def layer_kernel(
    peers, groups,
    hid_h, cot_h, wzx_h, wbc_h, wout_h, wdt_ref, gain_ref, cxw_ref, cxb_ref, cbw_ref, cbb_ref,
    dtb_ref, alog_ref, dsk_ref, ggain_ref,
    out_o, gh_o, gzx_o, gbc_o, gdt_o, min_o, pre_o, cb_o, gwo_o,
    hid, cot, wz, wx, wbc, wout, wdtp, hal, nx, ext, vec, slx, slbt, extt, cbwt, xh, bm, cm,
    tk, rows_t, tx, gx, wxs, outside, gat, gnm, ssd, gated, gs, gf, ggz, nout, gxa, gsc, gcum, csq,
    st, stat_s, stat_r, gpx, gpb, gbct, hb_r, sidet, wbct, wst, gcx, gcp,
    n_t, c_t, dec8, s_in, s_out, part_s, part_d, carry_in, carry_out, back_out,
    s1a, s1d, r1a, r1d, owna, ownd, s2a, s2d, r2a, r2d, accd, shr,
    pv, pr, po, pr2, hp, hr, hq, hr2, gmin, rm1, sm, rm2, smh,
    lsem, ss, rs, sc_s, sc_r, send1, recv1, send2, recv2, send_m, recv_m,
):
    me, g = lax.axis_index("seq"), lax.axis_index("head")
    pairs = peers // 2
    k, j = me // 2, me % 2
    length, width = hid.shape
    inner = xh.shape[1]
    heads = dec8.shape[0]
    hs = inner // heads
    states = bm.shape[1]
    hh = heads // 2
    part = width // peers
    half = length // 2
    share = wbc.shape[1] // groups
    full_inner = inner * groups
    partner = {"seq": me + 1 - 2 * j}
    diagonal = {"seq": (me + peers - 1 + 2 * j) % peers}
    ways = [{"head": (g + 1 + t) % groups} for t in range(groups - 1)]
    mate = {"head": g + 1 - 2 * (g % 2)}
    far = {"head": (g + 2) % groups}
    unroll = pairs <= 4

    def loop(count, body):
        if unroll:
            for t in range(count):
                body(t)
        else:
            pl.loop(0, count)(body)

    def zpeer(t):
        return {"seq": 2 * ((k + 1 + t) % pairs) + j}

    def remote(source, target, here, there, to):
        return pltpu.make_async_remote_copy(
            src_ref=source, dst_ref=target, send_sem=here, recv_sem=there,
            device_id=to, device_id_type=MESH,
        )

    def one(at, source, target, to):
        return remote(source, target, ss.at[at], rs.at[at], to)

    loads = [
        pltpu.make_async_copy(source, target, lsem.at[i])
        for i, (source, target) in enumerate((
            (hid_h, hid), (cot_h, cot), (wout_h, wout), (wzx_h.at[1], wx), (wbc_h, wbc),
            (wzx_h.at[0], wz),
        ))
    ]
    for copy in loads:
        copy.start()

    barrier = pltpu.get_barrier_semaphore()

    def greet(to):
        pl.semaphore_signal(barrier, inc=1, device_id=to, device_id_type=MESH)

    greet(partner)
    greet(diagonal)
    loop(pairs - 1, lambda t: greet(zpeer(t)))
    for to in ways:
        greet(to)

    wdtp[...] = jnp.zeros_like(wdtp)
    wdtp[0:heads] = wdt_ref[...]
    vec[...] = jnp.zeros_like(vec)
    vec[0:1, 0:heads] = dtb_ref[...]
    vec[1:2, 0:heads] = alog_ref[...]
    vec[2:3, 0:heads] = dsk_ref[...]
    st[...] = jnp.zeros_like(st)
    st[0:4] = cbw_ref[...]
    cbwt[...] = st[...].T
    st[...] = jnp.zeros_like(st)
    gmin[...] = jnp.zeros_like(gmin)
    sidet[...] = jnp.zeros_like(sidet)
    gain = gain_ref[...]
    ggain = ggain_ref[...]
    er = lax.broadcasted_iota(jnp.int32, (LANES, inner), 0) * hs
    ec = lax.broadcasted_iota(jnp.int32, (LANES, inner), 1)
    spread_m = jnp.where((ec >= er) & (ec < er + hs), 1.0, 0.0).astype(BF16)
    tr = lax.broadcasted_iota(jnp.int32, (inner, LANES), 1) * hs
    tc = lax.broadcasted_iota(jnp.int32, (inner, LANES), 0)
    gather_m = jnp.where((tc >= tr) & (tc < tr + hs), 1.0, 0.0).astype(BF16)
    ri = lax.broadcasted_iota(jnp.int32, (length, length), 0)
    ci = lax.broadcasted_iota(jnp.int32, (length, length), 1)
    lane = lax.broadcasted_iota(jnp.int32, (length, LANES), 1)

    def wide(value):
        return mm(value, spread_m, NN, 3)

    def narrow(value):
        return mm(value, gather_m, NN, 3)

    def rstd_of(values):
        return lax.rsqrt(jnp.mean(values * values, axis=-1, keepdims=True) + EPSILON)

    def normed_of(values):
        residual = values.astype(F32)
        return (residual * rstd_of(residual) * gain).astype(BF16)

    loads[0].wait()
    pl.semaphore_wait(barrier, pairs + groups)
    up = one(0, hid.at[pl.ds(length - HALO, HALO)], hal, {"seq": (me + 1) % peers})

    @pl.when(me < peers - 1)
    def _():
        up.start()

    @pl.when(me == 0)
    def _():
        hal[...] = jnp.zeros_like(hal)

    nx[HALO:] = normed_of(hid[...])
    loads[1].wait()
    loads[2].wait()
    gnm[...] = mm(cot[...], wout[...], NT)
    loads[3].wait()
    loads[4].wait()

    @pl.when(me > 0)
    def _():
        up.wait_recv()

    nx[0:HALO] = normed_of(hal[...])
    ext[:, 0:inner] = low(mm(nx[...], wx[...], NN))
    ext[:, inner:] = low(mm(nx[...], wbc[...], NN))
    dt_raw = mm(wdtp[...], nx[HALO:], NT).T
    z = dt_raw + vec[0:1]
    delta = softplus(z)
    rates = -jnp.exp(vec[1:2])
    tri = jnp.where(ri >= ci, 1.0, 0.0).astype(BF16)
    cum = mm(tri, delta * rates, NN, 1, 3)
    last = cum[length - 1 : length]
    tail_exp = jnp.exp(last - cum)
    tk[0] = cum
    tk[1] = delta
    tk[2] = tail_exp
    tk[3] = tail_exp * delta
    tk[4] = jnp.exp(cum)
    tk[5] = jax.nn.sigmoid(z)
    cum_t = cum.T
    rows_t[0] = cum_t[0:heads]
    rows_t[1] = delta.T[0:heads]
    dec8[...] = jnp.broadcast_to(jnp.exp(cum_t[0:heads, length - 1 : length]), dec8.shape)

    def conv(cols, weight, offset_b):
        total = offset_b + weight[0:1] * ext[HALO - 3 : HALO - 3 + length, cols]
        for at in range(1, 4):
            total = total + weight[at : at + 1] * ext[HALO - 3 + at : HALO - 3 + at + length, cols]
        return total

    pre_x = conv(slice(0, inner), cxw_ref[...], cxb_ref[...])
    sig_x = jax.nn.sigmoid(pre_x)
    xh[...] = (pre_x * sig_x).astype(BF16)
    slx[...] = sig_x * (1.0 + pre_x * (1.0 - sig_x))
    pre_bc = conv(slice(inner, inner + 2 * states), cbw_ref[...], cbb_ref[...])
    sig_bc = jax.nn.sigmoid(pre_bc)
    bc_post = pre_bc * sig_bc
    bm[...] = bc_post[:, :states].astype(BF16)
    cm[...] = bc_post[:, states:].astype(BF16)
    slbt[...] = (sig_bc * (1.0 + pre_bc * (1.0 - sig_bc))).T
    tx[...] = wide(tk[3])
    wxs[...] = tx[...] * xh[...].astype(F32)
    s_in[0] = mm(wxs[...].T, bm[...], NN, 2)

    class Scan:
        def __init__(self, way):
            self.way = way
            self.place = peers - 1 - me if way else me
            self.k, self.j = self.place // 2, self.place % 2
            self.mine = [
                pl.ds(pl.multiple_of((self.j * hh + c) * hs, hs), hs) for c in range(hh)
            ]
            theirs = [
                pl.ds(pl.multiple_of(((1 - self.j) * hh + c) * hs, hs), hs) for c in range(hh)
            ]
            onto = {"seq": (me + peers + (-2 if way else 2)) % peers}

            def copy(kind, c, source, target, to):
                return remote(source, target, sc_s.at[way, kind, c], sc_r.at[way, kind, c], to)

            self.give = [
                copy(0, c, s_in.at[way, theirs[c]], part_s.at[way, c], partner) for c in range(hh)
            ]
            self.give_d = copy(3, 0, dec8, part_d.at[way], partner)
            self.onward = [
                copy(1, c, carry_out.at[way, c], carry_in.at[way, c], onto) for c in range(hh)
            ]
            self.back = [
                copy(2, c, back_out.at[way, c], s_out.at[way, self.mine[c]], partner)
                for c in range(hh)
            ]

        def start(self):
            self.give_d.start()
            for copy in self.give:
                copy.start()

            @pl.when(self.k == 0)
            def _():
                carry_in[self.way] = jnp.zeros(carry_in.shape[1:], F32)

        def step(self):
            way = self.way
            early = self.j == 0
            self.give_d.wait()
            for c in range(hh):
                self.give[c].wait()
                row = pl.ds(self.j * hh + c, 1)
                own_s, own_d = s_in[way, self.mine[c]], dec8[row]
                got_s, got_d = part_s[way, c], part_d[way, row]
                s0, s1 = jnp.where(early, own_s, got_s), jnp.where(early, got_s, own_s)
                d0, d1 = jnp.where(early, own_d, got_d), jnp.where(early, got_d, own_d)

                @pl.when(self.k > 0)
                def _():
                    self.onward[c].wait_recv()

                before = carry_in[way, c]
                middle = d0 * before + s0

                @pl.when(self.k < pairs - 1)
                def _():
                    carry_out[way, c] = d1 * middle + s1
                    self.onward[c].start()

                back_out[way, c] = jnp.where(early, middle, before)
                self.back[c].start()
                s_out[way, self.mine[c]] = jnp.where(early, before, middle)

        def point(self, i, points):
            @pl.when(self.k == i if i < points - 1 else self.k >= i)
            def _():
                self.step()

        def finish(self):
            for c in range(hh):
                self.back[c].wait()

        def drain(self):
            @pl.when(self.k < pairs - 1)
            def _():
                for c in range(hh):
                    self.onward[c].wait_send()

    points = 4
    ahead = Scan(0)
    ahead.start()

    scores = mm(cm[...], bm[...], NT)
    scores_t = mm(bm[...], cm[...], NT)
    low_lane = lane < hs

    def decay_of(h):
        gap = tk[0, :, h : h + 1] - rows_t[0, h : h + 1, :]
        return jnp.exp(jnp.where(ri >= ci, gap, -jnp.inf))

    def inside_pair(q):
        cols = slice(q * LANES, (q + 1) * LANES)
        x_pair = xh[:, cols].astype(F32)
        total = None
        for side in range(2):
            h = 2 * q + side
            own = jnp.where(low_lane if side == 0 else ~low_lane, x_pair, 0.0).astype(BF16)
            weights = scores * decay_of(h) * rows_t[1, h : h + 1, :]
            term = mm(weights, own, NN, 2)
            total = term if total is None else total + term
        ssd[:, cols] = total

    ahead.point(0, points)
    loads[5].wait()
    gat[...] = mm(nx[HALO:], wz[...], NN)
    inside_pair(0)
    ahead.point(1, points)
    inside_pair(1)
    inside_pair(2)
    ahead.point(2, points)
    inside_pair(3)

    def turned(values, target):
        value = values.astype(F32).T.astype(BF16)
        for owner in range(peers):
            target[owner % 2, owner // 2 * part : (owner // 2 + 1) * part] = (
                value[owner * part : (owner + 1) * part]
            )

    turned(cot[...], c_t)
    ahead.point(3, points)
    turned(nx[HALO:], n_t)
    ahead.finish()

    x_all = xh[...].astype(F32)
    gx[...] = wide(tk[4])
    outside[...] = gx[...] * mm(cm[...], s_out[0], NT, 1, 2)
    skip_w = mm(vec[...], spread_m, NN, 3)[2:3]
    ssd[...] = ssd[...] + outside[...] + skip_w * x_all
    act = gat[...] * jax.nn.sigmoid(gat[...])
    gated[...] = ssd[...] * act
    scaled = gnm[...] * ggain
    q1 = jnp.sum(gated[...] * gated[...], axis=-1, keepdims=True)
    q2 = jnp.sum(scaled * gated[...], axis=-1, keepdims=True)
    packed = jnp.where(lane == 0, q1, jnp.where(lane == 1, q2, 0.0))
    stat_s[...] = packed.T[0:8]
    stats = [one(1 + t, stat_s, stat_r.at[t], ways[t]) for t in range(groups - 1)]
    for copy in stats:
        copy.start()
    for at in range(4):
        extt[at] = ext[HALO - 3 + at : HALO - 3 + at + length, inner:].T
    wbct[...] = wbc[...].astype(F32).T.astype(BF16)
    wst[...] = jnp.zeros_like(wst)
    wst[0:share] = wbct[pl.ds(pl.multiple_of(g * share, share), share)]
    wst[share : share + 16] = wdtp[0:16]
    for copy in stats:
        copy.wait()
    total = stat_s[...]
    for t in range(groups - 1):
        total = total + stat_r[t]
    st[0:8] = total
    cols = st[...].T
    rstd = lax.rsqrt(cols[:, 0:1] / full_inner + EPSILON)
    mean_dot = cols[:, 1:2] / full_inner
    sig_g = jax.nn.sigmoid(gat[...])
    act = gat[...] * sig_g
    scaled = gnm[...] * ggain
    grad_gated = rstd * scaled - gated[...] * (rstd * rstd * rstd * mean_dot)
    gs[...] = grad_gated * act
    gf[...] = gx[...] * gs[...]
    s_in[1] = mm(gf[...].T, cm[...], NN, 2)
    behind = Scan(1)
    behind.start()
    behind.point(0, points)
    nout[...] = (gated[...] * rstd * ggain).astype(BF16)

    def rs_first(ph, t):
        kk = (k + 1 + t) % pairs
        rows = pl.ds(pl.multiple_of(kk * part, part), part)
        s1, r1 = (s1a.at[ph], r1a.at[ph]) if ph < 3 else (s1d, r1d)
        return remote(s1.at[rows], r1.at[rows], send1.at[ph, t], recv1.at[ph, t], partner)

    def rs_give(ph, left, right):
        give = mm(left[1 - j], right, NN).astype(BF16)
        if ph < 3:
            s1a[ph] = give
        else:
            s1d[...] = give
        loop(pairs, lambda t: rs_first(ph, t).start())

    def rs_own(ph, left, right):
        keep = mm(left[j], right, NN)
        if ph < 3:
            owna[ph] = keep
        else:
            ownd[...] = keep

    def rs_second(ph, t):
        s2, r2 = (s2a.at[ph, t], r2a.at[ph, t]) if ph < 3 else (s2d.at[t], r2d.at[t])
        return remote(s2, r2, send2.at[ph, t], recv2.at[ph, t], zpeer(t))

    def rs_join(ph, t):
        rs_first(ph, t).wait()
        rows = pl.ds(pl.multiple_of(((k + 1 + t) % pairs) * part, part), part)
        if ph < 3:
            return owna[ph, rows] + r1a[ph, rows].astype(F32)
        return ownd[rows] + r1d[rows].astype(F32)

    def rs_mid(ph):
        def pass_on(t):
            value = rs_join(ph, t).astype(BF16)
            if ph < 3:
                s2a[ph, t] = value
            else:
                s2d[t] = value
            rs_second(ph, t).start()

        loop(pairs - 1, pass_on)

    def rs_end(ph, target):
        target[...] = rs_join(ph, pairs - 1)

        def collect(t):
            rs_second(ph, t).wait()
            target[...] += (r2a[ph, t] if ph < 3 else r2d[t]).astype(F32)

        loop(pairs - 1, collect)

    rs_give(0, c_t, nout[...])
    pv[...] = mm(nout[...], wout[...], NN)
    my_half = pl.ds(pl.multiple_of((g % 2) * half, half), half)
    other_half = pl.ds(pl.multiple_of((1 - g % 2) * half, half), half)
    out_give = one(4, pv.at[other_half], pr, mate)
    out_give.start()
    sig_g = jax.nn.sigmoid(gat[...])
    slope_g = sig_g * (1.0 + gat[...] * (1.0 - sig_g))
    grad_gated = rstd * (gnm[...] * ggain) - gated[...] * (rstd * rstd * rstd * mean_dot)
    ggz[...] = (grad_gated * ssd[...] * slope_g).astype(BF16)
    gmin[5:6] = jnp.sum(gnm[...] * gated[...] * rstd, axis=0, keepdims=True)
    behind.point(1, points)
    rs_give(1, n_t, ggz[...])
    rs_own(0, c_t, nout[...])
    rs_own(1, n_t, ggz[...])

    gxa[...] = skip_w * gs[...]
    gmin[14:15] = jnp.sum(gs[...] * xh[...].astype(F32), axis=0, keepdims=True)
    gsc[...] = jnp.zeros_like(gsc)
    gcum[...] = narrow(gs[...] * outside[...])

    def back_pair(q):
        cols = slice(q * LANES, (q + 1) * LANES)
        x_pair = xh[:, cols]
        g_pair = gs[:, cols]
        total = None
        for side in range(2):
            h = 2 * q + side
            own = jnp.where(low_lane if side == 0 else ~low_lane, g_pair, 0.0)
            own_hi, own_lo = split(own, 2)
            grad_w = mm(own_hi, x_pair, NT) + mm(own_lo, x_pair, NT)
            d_row = rows_t[1, h : h + 1, :]
            plain = grad_w * decay_of(h)
            gsc[...] += plain * d_row
            inner_w = plain * scores
            csq[h : h + 1, :] = jnp.sum(inner_w, axis=0, keepdims=True)
            gcum[...] += jnp.where(
                lane == h, jnp.sum(inner_w * d_row, axis=1, keepdims=True), 0.0
            )
            gap_t = rows_t[0, h : h + 1, :] - tk[0, :, h : h + 1]
            w_t = scores_t * jnp.exp(jnp.where(ci >= ri, gap_t, -jnp.inf)) * tk[1, :, h : h + 1]
            w_hi, w_lo = split(w_t, 2)
            term = mm(w_hi, own_hi, NN) + mm(w_hi, own_lo, NN) + mm(w_lo, own_hi, NN)
            total = term if total is None else total + term
        gxa[:, cols] += total

    back_pair(0)
    behind.point(2, points)
    back_pair(1)
    back_pair(2)
    behind.point(3, points)
    rs_mid(0)
    out_give.wait()
    po[...] = pv[my_half] + pr[...]
    out_far = one(5, po, pr2, far)
    out_far.start()
    back_pair(3)
    gcp[...] = mm(gf[...], s_out[0], NN, 2, 2) + mm(gsc[...], bm[...], NN, 2)
    gbp = mm(gsc[...].T, cm[...], NN, 2)
    behind.finish()

    gw = mm(bm[...], s_out[1], NT, 1, 2)
    gpx[0:length] = (gxa[...] + tx[...] * gw) * slx[...]
    down = one(6, gpx.at[pl.ds(0, 8)], gpx.at[pl.ds(length, 8)], {"seq": (me + peers - 1) % peers})

    @pl.when(me > 0)
    def _():
        down.start()

    @pl.when(me == peers - 1)
    def _():
        gpx[length : length + 8] = jnp.zeros((8, inner), F32)
        gpb[:, length:] = jnp.zeros((share, LANES), F32)

    gbp = gbp + mm(wxs[...], s_out[1], NN, 2, 2)
    gbct[0:states] = gbp.T
    gbct[states:] = gcp[...].T

    def share_of(owner):
        return pl.ds(pl.multiple_of(owner * share, share), share)

    bc_gives = [
        one(7 + t, gbct.at[share_of((g + 1 + t) % groups)], hb_r.at[t], ways[t])
        for t in range(groups - 1)
    ]
    for copy in bc_gives:
        copy.start()

    grad_tail = narrow(gw * xh[...].astype(F32))
    tail_part = grad_tail * tk[3]
    st[0:8] = csq[...]
    csq_t = st[...].T
    grad_cum = gcum[...] - csq_t * tk[1] - tail_part
    grad_delta = grad_tail * tk[2] + csq_t
    prod = mm(spread_m, s_out[1] * s_out[0], NN, 1, 3)
    per_head = jnp.sum(prod, axis=1, keepdims=True)
    eye_r = lax.broadcasted_iota(jnp.int32, (LANES, LANES), 0)
    eye_c = lax.broadcasted_iota(jnp.int32, (LANES, LANES), 1)
    state_dot = jnp.sum(jnp.where(eye_r == eye_c, per_head, 0.0), axis=0, keepdims=True)
    growth_last = tk[4, length - 1 : length]
    grad_last = state_dot * growth_last + jnp.sum(tail_part, axis=0, keepdims=True)
    tri_t = jnp.where(ci >= ri, 1.0, 0.0).astype(BF16)
    grad_log = mm(tri_t, grad_cum, NN, 1, 3) + grad_last
    rates = -jnp.exp(vec[1:2])
    grad_u = (grad_delta + grad_log * rates) * tk[5]
    gmin[6:7, 0:LANES] = jnp.sum(grad_u, axis=0, keepdims=True)
    gmin[6:7, LANES : 2 * LANES] = rates * jnp.sum(grad_log * tk[1], axis=0, keepdims=True)
    gmin[6:7, 2 * LANES : 3 * LANES] = narrow(gmin[8:16])[6:7]
    gmin[14:15] = jnp.zeros((1, inner), F32)
    sidet[share : share + 8] = grad_u.T[0:8]

    @pl.when(me < peers - 1)
    def _():
        down.wait_recv()

    grad_in = None
    for at in range(4):
        term = cxw_ref[at : at + 1] * gpx[3 - at : 3 - at + length]
        grad_in = term if grad_in is None else grad_in + term
    gcx[...] = grad_in.astype(BF16)
    rs_give(2, n_t, gcx[...])

    for copy in bc_gives:
        copy.wait()
    gp = gbct[share_of(g)]
    for t in range(groups - 1):
        gp = gp + hb_r[t]
    gp = gp * slbt[share_of(g)]
    gpb[:, 0:length] = gp
    down_bc = one(
        10, gpb.at[:, pl.ds(0, LANES)], gpb.at[:, pl.ds(length, LANES)],
        {"seq": (me + peers - 1) % peers},
    )

    @pl.when(me > 0)
    def _():
        down_bc.start()

    hp[...] = mm(ggz[...], wz[...], NT) + mm(gcx[...], wx[...], NT)
    rs_own(2, n_t, gcx[...])
    for at in range(4):
        gmin[at : at + 1] = jnp.sum(
            gpx[0:length] * ext[HALO - 3 + at : HALO - 3 + at + length, 0:inner],
            axis=0, keepdims=True,
        )
    gmin[4:5] = jnp.sum(gpx[0:length], axis=0, keepdims=True)
    lane_s = lax.broadcasted_iota(jnp.int32, (LANES, LANES), 1)[0:share]
    conv_cols = jnp.where(lane_s == 4, jnp.sum(gp, axis=1, keepdims=True), 0.0)
    for at in range(4):
        conv_cols = jnp.where(
            lane_s == at, jnp.sum(gp * extt[at, share_of(g)], axis=1, keepdims=True), conv_cols
        )
    conv_cols = jnp.concatenate([conv_cols, jnp.zeros((LANES - share, LANES), F32)], axis=0)
    gmin[9:14, 0:LANES] = conv_cols.T[0:5]

    @pl.when(me < peers - 1)
    def _():
        down_bc.wait_recv()

    ge = gpb[...]
    taps = cbwt[share_of(g)]
    total = None
    for at in range(4):
        moved = ge if at == 3 else pltpu.roll(ge, length + LANES - (3 - at), 1)
        term = taps[:, at : at + 1] * moved[:, 0:length]
        total = term if total is None else total + term
    sidet[0:share] = total
    side = sidet[...].T.astype(BF16)
    rs_give(3, n_t, side)
    hp[...] += mm(side, wst[...], NN)
    hp_give = one(11, hp.at[other_half], hr, mate)
    hp_give.start()
    residual = hid[...].astype(F32)
    pre = jnp.sum(hp[...] * (residual * rstd_of(residual)), axis=0, keepdims=True)
    for at in range(width // inner):
        gmin[7 + at : 8 + at] = pre[:, at * inner : (at + 1) * inner]
    minor_first = remote(gmin, rm1, send_m.at[pairs], recv_m.at[pairs], partner)
    minor_first.start()
    rs_own(3, n_t, side)
    rs_mid(1)

    out_far.wait()
    out_o[my_half] = (hid[my_half].astype(F32) + (po[...] + pr2[...])).astype(BF16)
    out_back = one(12, out_o.at[my_half], out_o.at[my_half], mate)
    out_back.start()

    hp_give.wait()
    hq[...] = (hp[my_half] + hr[...]).astype(BF16)
    hp_far = one(13, hq, hr2, far)
    hp_far.start()
    minor_first.wait()
    sm[...] = gmin[...] + rm1[...]

    def minor_second(t):
        return remote(sm, rm2.at[t], send_m.at[t], recv_m.at[t], zpeer(t))

    loop(pairs - 1, lambda t: minor_second(t).start())
    rs_mid(2)
    rs_mid(3)
    hp_far.wait()
    grad_normed_in = hq[...].astype(F32) + hr2[...].astype(F32)
    residual = hid[my_half].astype(F32)
    in_rstd = rstd_of(residual)
    scaled_in = grad_normed_in * gain
    gh_o[my_half] = (
        cot[my_half].astype(F32)
        + in_rstd * scaled_in
        - residual
        * (in_rstd * in_rstd * in_rstd)
        * jnp.mean(scaled_in * residual, axis=-1, keepdims=True)
    )
    gh_back = one(14, gh_o.at[my_half], gh_o.at[my_half], mate)
    gh_back.start()
    loop(pairs - 1, lambda t: minor_second(t).wait())

    def ordered(q, total):
        slot = (k - q + pairs - 1) % pairs
        value = jnp.where(slot == pairs - 1, sm[...], rm2[jnp.minimum(slot, pairs - 2)])
        return total + value

    smh[g] = lax.fori_loop(0, pairs, ordered, jnp.zeros(sm.shape, F32))
    minor_heads = [one(15 + t, smh.at[g], smh.at[g], ways[t]) for t in range(groups - 1)]
    for copy in minor_heads:
        copy.start()
    min_o[...] = smh[g]
    rs_end(3, accd)
    shr[g] = accd[...]
    shares = [one(18 + t, shr.at[g], shr.at[g], ways[t]) for t in range(groups - 1)]
    for copy in shares:
        copy.start()
    rs_end(0, owna.at[0, pl.ds(0, part)])
    gwo_o[...] = owna[0, 0:part].T
    rs_end(1, gzx_o.at[:, pl.ds(0, inner)])
    gdt_o[...] = accd[...].T[share : share + heads]
    for copy in minor_heads:
        copy.wait()
    pre_sum = smh[0]
    for q in range(1, groups):
        pre_sum = pre_sum + smh[q]
    for at in range(width // inner):
        pre_o[:, at * inner : (at + 1) * inner] = pre_sum[7 + at : 8 + at]
    for q in range(groups // 2):
        left = smh[2 * q, 8:16, 0:LANES]
        right = pltpu.roll(smh[2 * q + 1, 8:16, 0:LANES], share, 1)
        cb_o[:, q * LANES : (q + 1) * LANES] = jnp.where(lane[0:8] < share, left, right)
    rs_end(2, gzx_o.at[:, pl.ds(inner, inner)])
    for copy in shares:
        copy.wait()
    for q in range(groups // 2):
        right = pltpu.roll(shr[2 * q + 1], share, 1)
        gbc_o[:, q * LANES : (q + 1) * LANES] = jnp.where(lane[0:part] < share, shr[2 * q], right)

    out_back.wait()
    gh_back.wait()
    ahead.drain()
    behind.drain()

    @pl.when(me < peers - 1)
    def _():
        up.wait_send()

    @pl.when(me > 0)
    def _():
        down.wait_send()
        down_bc.wait_send()


def on_device(
    hidden, cotangent, pre_gain, w_zx, w_bc, w_dt, conv_x_w, conv_x_b, conv_bc_w, conv_bc_b,
    dt_bias, a_log, d_skip, gate_gain, w_out,
):
    peers, groups = lax.axis_size("seq"), lax.axis_size("head")
    pairs = peers // 2
    length, width = hidden.shape[1:]
    heads = dt_bias.shape[0]
    inner = w_zx.shape[2]
    hs = inner // heads
    bc = w_bc.shape[1]
    states = bc // 2
    share = bc // groups
    part = width // peers
    half = length // 2
    hh = heads // 2

    def row(value):
        return value.reshape(1, -1)

    def f32(*shape):
        return VMEM(shape, F32)

    def b16(*shape):
        return VMEM(shape, BF16)

    shapes = (
        ((length, width), BF16), ((length, width), F32), ((part, 2 * inner), F32),
        ((part, bc), F32), ((heads, part), F32), ((16, inner), F32), ((1, width), F32),
        ((8, bc), F32), ((inner, part), F32),
    )
    scratch = [
        b16(length, width), b16(length, width), b16(width, inner), b16(width, inner),
        b16(width, bc), b16(inner, width), b16(LANES, width),
        b16(HALO, width), b16(HALO + length, width), f32(HALO + length, inner + bc), f32(8, LANES),
        f32(length, inner), f32(bc, length), f32(4, bc, length), f32(bc, LANES),
        b16(length, inner), b16(length, states), b16(length, states),
        f32(6, length, LANES), f32(2, heads, length),
        f32(length, inner), f32(length, inner), f32(length, inner), f32(length, inner),
        f32(length, inner), f32(length, inner), f32(length, inner), f32(length, inner),
        f32(length, inner), f32(length, inner), b16(length, inner), b16(length, inner),
        f32(length, inner), f32(length, length), f32(length, LANES), f32(heads, length),
        f32(LANES, length), f32(8, length), f32(groups - 1, 8, length),
        f32(length + 8, inner), f32(share, length + LANES), f32(bc, length),
        f32(groups - 1, share, length), f32(LANES, length), b16(bc, width), b16(LANES, width),
        b16(length, inner), f32(length, states),
        b16(2, width // 2, length), b16(2, width // 2, length),
        f32(heads, LANES), f32(2, inner, states), f32(2, inner, states),
        f32(2, hh, hs, states), f32(2, heads, LANES), f32(2, hh, hs, states),
        f32(2, hh, hs, states), f32(2, hh, hs, states),
        b16(3, width // 2, inner), b16(width // 2, LANES),
        b16(3, width // 2, inner), b16(width // 2, LANES),
        f32(3, width // 2, inner), f32(width // 2, LANES),
        b16(3, pairs - 1, part, inner), b16(pairs - 1, part, LANES),
        b16(3, pairs - 1, part, inner), b16(pairs - 1, part, LANES),
        f32(part, LANES), f32(groups, part, LANES),
        f32(length, width), f32(half, width), f32(half, width), f32(half, width),
        f32(length, width), f32(half, width), b16(half, width), b16(half, width),
        f32(16, inner), f32(16, inner), f32(16, inner), f32(pairs - 1, 16, inner),
        f32(groups, 16, inner),
        DMA((6,)), DMA((21,)), DMA((21,)), DMA((2, 4, hh)), DMA((2, 4, hh)),
        DMA((4, pairs)), DMA((4, pairs)), DMA((4, pairs)), DMA((4, pairs)),
        DMA((pairs + 1,)), DMA((pairs + 1,)),
    ]
    output, grad_hidden, g_zx, g_bc, g_dt, minor, g_pre, g_cb, g_out = pl.pallas_call(
        functools.partial(layer_kernel, peers, groups),
        out_shape=tuple(jax.ShapeDtypeStruct(*s) for s in shapes),
        in_specs=[ANYWHERE] * 5 + [IN_VMEM] * 10,
        out_specs=(IN_VMEM,) * len(shapes),
        scratch_shapes=scratch,
        compiler_params=pltpu.CompilerParams(
            collective_id=1, has_side_effects=True, vmem_limit_bytes=60 * 2**20
        ),
        cost_estimate=pl.CostEstimate(flops=5 * 10**9, bytes_accessed=10**7, transcendentals=0),
        name="layer",
    )(
        hidden[0], cotangent[0], w_zx.transpose(1, 0, 2), w_bc, w_out, w_dt.T, row(pre_gain),
        conv_x_w, row(conv_x_b), conv_bc_w, row(conv_bc_b), row(dt_bias), row(a_log), row(d_skip),
        row(gate_gain),
    )
    return (
        output[None],
        grad_hidden[None],
        g_pre.reshape(-1),
        g_zx.reshape(part, 2, inner),
        g_bc,
        g_dt.T,
        minor[0:4],
        minor[4],
        g_cb[1:5],
        g_cb[5],
        minor[6, 0:heads],
        minor[6, LANES : LANES + heads],
        minor[6, 2 * LANES : 2 * LANES + heads],
        minor[5],
        g_out,
    )


def solution(mesh):
    return jax.shard_map(
        on_device,
        mesh=mesh,
        in_specs=(
            P(None, "seq", None), P(None, "seq", None), P(), P(None, None, "head"), P(),
            P(None, "head"), P(None, "head"), P("head"), P(), P(), P("head"), P("head"), P("head"),
            P("head"), P("head", None),
        ),
        out_specs=(
            P(None, "seq", None), P(None, "seq", None), P(), P("seq", None, "head"),
            P("seq", None), P("seq", "head"), P(None, "head"), P("head"), P(), P(), P("head"),
            P("head"), P("head"), P("head"), P("head", "seq"),
        ),
        check_vma=False,
    )
```

```python
import functools

import jax
import jax.numpy as jnp
from jax import lax
from jax.experimental import pallas as pl
from jax.experimental.pallas import tpu as pltpu
from jax.sharding import PartitionSpec as P

MESH = pl.DeviceIdType.MESH
VMEM = pltpu.VMEM
DMA = pltpu.SemaphoreType.DMA
IN_VMEM = pl.BlockSpec(memory_space=pltpu.VMEM)
ANYWHERE = pl.BlockSpec(memory_space=pl.ANY)

EPSILON = 1e-05
HALO = 16
LANES = 128
BF16, F32 = jnp.bfloat16, jnp.float32
NN, NT = ((1,), (0,)), ((1,), (1,))


def split(value, parts):
    if value.dtype == BF16:
        return [value]
    terms = []
    for at in range(parts):
        terms.append(value.astype(BF16))
        if at < parts - 1:
            value = value - terms[-1].astype(F32)
    return terms


def mm(left, right, dims, left_parts=1, right_parts=1):
    total = None
    most = max(left_parts, right_parts)
    rights = split(right, right_parts)
    for i, a in enumerate(split(left, left_parts)):
        for k, b in enumerate(rights):
            if i + k < most:
                term = lax.dot_general(a, b, (dims, ((), ())), preferred_element_type=F32)
                total = term if total is None else total + term
    return total


def low(values):
    return values.astype(BF16).astype(F32)


def softplus(values):
    return jnp.maximum(values, 0.0) + jnp.log1p(jnp.exp(-jnp.abs(values)))


def layer_kernel(
    peers, groups,
    hid_h, cot_h, wzx_h, wbc_h, wout_h, wdt_ref, gain_ref, cxw_ref, cxb_ref, cbw_ref, cbb_ref,
    dtb_ref, alog_ref, dsk_ref, ggain_ref,
    out_o, gh_o, gzx_o, gbc_o, gdt_o, min_o, pre_o, cb_o, gwo_o,
    hid, cot, wz, wx, wbc, wout, wdtp, hal, nx, ext, vec, slx, slbt, extt, cbwt, xh, bm, cm,
    tk, rows_t, tx, gx, wxs, outside, gat, gnm, ssd, gated, gs, gf, ggz, nout, gxa, gsc, gcum, csq,
    st, stat_s, stat_r, gpx, gpb, gbct, hb_r, sidet, wbct, wst, gcx, gcp,
    n_t, c_t, n_p, c_p, sidev, dec8, s_in, s_out, part_s, part_d, carry_in, carry_out, back_out,
    rpa, rpd, owna, ownd, s2a, s2d, r2a, r2d, accd, shr,
    pv, pr, po, pr2, hp, hr, hq, hr2, gmin, rm1, sm, rm2, smh,
    lsem, ss, rs, sc_s, sc_r, send1, recv1, send2, recv2, send_m, recv_m,
):
    me, g = lax.axis_index("seq"), lax.axis_index("head")
    pairs = peers // 2
    k, j = me // 2, me % 2
    length, width = hid.shape
    inner = xh.shape[1]
    heads = dec8.shape[0]
    hs = inner // heads
    states = bm.shape[1]
    hh = heads // 2
    part = width // peers
    half = length // 2
    share = wbc.shape[1] // groups
    full_inner = inner * groups
    partner = {"seq": me + 1 - 2 * j}
    diagonal = {"seq": (me + peers - 1 + 2 * j) % peers}
    ways = [{"head": (g + 1 + t) % groups} for t in range(groups - 1)]
    mate = {"head": g + 1 - 2 * (g % 2)}
    far = {"head": (g + 2) % groups}
    unroll = pairs <= 4

    def loop(count, body):
        if unroll:
            for t in range(count):
                body(t)
        else:
            pl.loop(0, count)(body)

    def zpeer(t):
        return {"seq": 2 * ((k + 1 + t) % pairs) + j}

    def remote(source, target, here, there, to):
        return pltpu.make_async_remote_copy(
            src_ref=source, dst_ref=target, send_sem=here, recv_sem=there,
            device_id=to, device_id_type=MESH,
        )

    def one(at, source, target, to):
        return remote(source, target, ss.at[at], rs.at[at], to)

    loads = [
        pltpu.make_async_copy(source, target, lsem.at[i])
        for i, (source, target) in enumerate((
            (hid_h, hid), (cot_h, cot), (wout_h, wout), (wzx_h.at[1], wx), (wbc_h, wbc),
            (wzx_h.at[0], wz),
        ))
    ]
    for copy in loads:
        copy.start()

    barrier = pltpu.get_barrier_semaphore()

    def greet(to):
        pl.semaphore_signal(barrier, inc=1, device_id=to, device_id_type=MESH)

    greet(partner)
    greet(diagonal)
    loop(pairs - 1, lambda t: greet(zpeer(t)))
    for to in ways:
        greet(to)

    wdtp[...] = jnp.zeros_like(wdtp)
    wdtp[0:heads] = wdt_ref[...]
    vec[...] = jnp.zeros_like(vec)
    vec[0:1, 0:heads] = dtb_ref[...]
    vec[1:2, 0:heads] = alog_ref[...]
    vec[2:3, 0:heads] = dsk_ref[...]
    st[...] = jnp.zeros_like(st)
    st[0:4] = cbw_ref[...]
    cbwt[...] = st[...].T
    st[...] = jnp.zeros_like(st)
    gmin[...] = jnp.zeros_like(gmin)
    sidet[...] = jnp.zeros_like(sidet)
    gain = gain_ref[...]
    ggain = ggain_ref[...]
    er = lax.broadcasted_iota(jnp.int32, (LANES, inner), 0) * hs
    ec = lax.broadcasted_iota(jnp.int32, (LANES, inner), 1)
    spread_m = jnp.where((ec >= er) & (ec < er + hs), 1.0, 0.0).astype(BF16)
    tr = lax.broadcasted_iota(jnp.int32, (inner, LANES), 1) * hs
    tc = lax.broadcasted_iota(jnp.int32, (inner, LANES), 0)
    gather_m = jnp.where((tc >= tr) & (tc < tr + hs), 1.0, 0.0).astype(BF16)
    ri = lax.broadcasted_iota(jnp.int32, (length, length), 0)
    ci = lax.broadcasted_iota(jnp.int32, (length, length), 1)
    lane = lax.broadcasted_iota(jnp.int32, (length, LANES), 1)

    def wide(value):
        return mm(value, spread_m, NN, 3)

    def narrow(value):
        return mm(value, gather_m, NN, 3)

    def rstd_of(values):
        return lax.rsqrt(jnp.mean(values * values, axis=-1, keepdims=True) + EPSILON)

    def normed_of(values):
        residual = values.astype(F32)
        return (residual * rstd_of(residual) * gain).astype(BF16)

    loads[0].wait()
    pl.semaphore_wait(barrier, pairs + groups)
    up = one(0, hid.at[pl.ds(length - HALO, HALO)], hal, {"seq": (me + 1) % peers})

    @pl.when(me < peers - 1)
    def _():
        up.start()

    @pl.when(me == 0)
    def _():
        hal[...] = jnp.zeros_like(hal)

    def turned(values, target):
        value = values.astype(F32).T.astype(BF16)
        for owner in range(peers):
            target[owner % 2, owner // 2 * part : (owner // 2 + 1) * part] = (
                value[owner * part : (owner + 1) * part]
            )

    nx[HALO:] = normed_of(hid[...])
    loads[1].wait()
    turned(cot[...], c_t)
    c_give = one(21, c_t.at[1 - j], c_p, partner)
    c_give.start()
    loads[3].wait()
    loads[4].wait()

    @pl.when(me > 0)
    def _():
        up.wait_recv()

    nx[0:HALO] = normed_of(hal[...])
    ext[:, 0:inner] = low(mm(nx[...], wx[...], NN))
    ext[:, inner:] = low(mm(nx[...], wbc[...], NN))
    dt_raw = mm(wdtp[...], nx[HALO:], NT).T
    z = dt_raw + vec[0:1]
    delta = softplus(z)
    rates = -jnp.exp(vec[1:2])
    tri = jnp.where(ri >= ci, 1.0, 0.0).astype(BF16)
    cum = mm(tri, delta * rates, NN, 1, 3)
    last = cum[length - 1 : length]
    tail_exp = jnp.exp(last - cum)
    tk[0] = cum
    tk[1] = delta
    tk[2] = tail_exp
    tk[3] = tail_exp * delta
    tk[4] = jnp.exp(cum)
    tk[5] = jax.nn.sigmoid(z)
    cum_t = cum.T
    rows_t[0] = cum_t[0:heads]
    rows_t[1] = delta.T[0:heads]
    dec8[...] = jnp.broadcast_to(jnp.exp(cum_t[0:heads, length - 1 : length]), dec8.shape)

    def conv(cols, weight, offset_b):
        total = offset_b + weight[0:1] * ext[HALO - 3 : HALO - 3 + length, cols]
        for at in range(1, 4):
            total = total + weight[at : at + 1] * ext[HALO - 3 + at : HALO - 3 + at + length, cols]
        return total

    pre_x = conv(slice(0, inner), cxw_ref[...], cxb_ref[...])
    sig_x = jax.nn.sigmoid(pre_x)
    xh[...] = (pre_x * sig_x).astype(BF16)
    slx[...] = sig_x * (1.0 + pre_x * (1.0 - sig_x))
    pre_bc = conv(slice(inner, inner + 2 * states), cbw_ref[...], cbb_ref[...])
    sig_bc = jax.nn.sigmoid(pre_bc)
    bc_post = pre_bc * sig_bc
    bm[...] = bc_post[:, :states].astype(BF16)
    cm[...] = bc_post[:, states:].astype(BF16)
    slbt[...] = (sig_bc * (1.0 + pre_bc * (1.0 - sig_bc))).T
    tx[...] = wide(tk[3])
    wxs[...] = tx[...] * xh[...].astype(F32)
    s_in[0] = mm(wxs[...].T, bm[...], NN, 2)

    class Scan:
        def __init__(self, way):
            self.way = way
            self.place = peers - 1 - me if way else me
            self.k, self.j = self.place // 2, self.place % 2
            self.mine = [
                pl.ds(pl.multiple_of((self.j * hh + c) * hs, hs), hs) for c in range(hh)
            ]
            theirs = [
                pl.ds(pl.multiple_of(((1 - self.j) * hh + c) * hs, hs), hs) for c in range(hh)
            ]
            onto = {"seq": (me + peers + (-2 if way else 2)) % peers}

            def copy(kind, c, source, target, to):
                return remote(source, target, sc_s.at[way, kind, c], sc_r.at[way, kind, c], to)

            self.give = [
                copy(0, c, s_in.at[way, theirs[c]], part_s.at[way, c], partner) for c in range(hh)
            ]
            self.give_d = copy(3, 0, dec8, part_d.at[way], partner)
            self.onward = [
                copy(1, c, carry_out.at[way, c], carry_in.at[way, c], onto) for c in range(hh)
            ]
            self.back = [
                copy(2, c, back_out.at[way, c], s_out.at[way, self.mine[c]], partner)
                for c in range(hh)
            ]

        def start(self):
            self.give_d.start()
            for copy in self.give:
                copy.start()

            @pl.when(self.k == 0)
            def _():
                carry_in[self.way] = jnp.zeros(carry_in.shape[1:], F32)

        def step(self):
            way = self.way
            early = self.j == 0
            self.give_d.wait()
            for c in range(hh):
                self.give[c].wait()
                row = pl.ds(self.j * hh + c, 1)
                own_s, own_d = s_in[way, self.mine[c]], dec8[row]
                got_s, got_d = part_s[way, c], part_d[way, row]
                s0, s1 = jnp.where(early, own_s, got_s), jnp.where(early, got_s, own_s)
                d0, d1 = jnp.where(early, own_d, got_d), jnp.where(early, got_d, own_d)

                @pl.when(self.k > 0)
                def _():
                    self.onward[c].wait_recv()

                before = carry_in[way, c]
                middle = d0 * before + s0

                @pl.when(self.k < pairs - 1)
                def _():
                    carry_out[way, c] = d1 * middle + s1
                    self.onward[c].start()

                back_out[way, c] = jnp.where(early, middle, before)
                self.back[c].start()
                s_out[way, self.mine[c]] = jnp.where(early, before, middle)

        def point(self, i, points):
            @pl.when(self.k == i if i < points - 1 else self.k >= i)
            def _():
                self.step()

        def finish(self):
            for c in range(hh):
                self.back[c].wait()

        def drain(self):
            @pl.when(self.k < pairs - 1)
            def _():
                for c in range(hh):
                    self.onward[c].wait_send()

    points = 4
    ahead = Scan(0)
    ahead.start()

    scores = mm(cm[...], bm[...], NT)
    scores_t = mm(bm[...], cm[...], NT)
    low_lane = lane < hs

    def decay_of(h):
        gap = tk[0, :, h : h + 1] - rows_t[0, h : h + 1, :]
        return jnp.exp(jnp.where(ri >= ci, gap, -jnp.inf))

    def inside_pair(q):
        cols = slice(q * LANES, (q + 1) * LANES)
        x_pair = xh[:, cols].astype(F32)
        total = None
        for side in range(2):
            h = 2 * q + side
            own = jnp.where(low_lane if side == 0 else ~low_lane, x_pair, 0.0).astype(BF16)
            weights = scores * decay_of(h) * rows_t[1, h : h + 1, :]
            term = mm(weights, own, NN, 2)
            total = term if total is None else total + term
        ssd[:, cols] = total

    ahead.point(0, points)
    loads[5].wait()
    gat[...] = mm(nx[HALO:], wz[...], NN)
    inside_pair(0)
    ahead.point(1, points)
    inside_pair(1)
    inside_pair(2)
    ahead.point(2, points)
    inside_pair(3)
    loads[2].wait()
    gnm[...] = mm(cot[...], wout[...], NT)

    ahead.point(3, points)
    turned(nx[HALO:], n_t)
    ahead.finish()
    n_give = one(22, n_t.at[1 - j], n_p, partner)
    n_give.start()

    x_all = xh[...].astype(F32)
    gx[...] = wide(tk[4])
    outside[...] = gx[...] * mm(cm[...], s_out[0], NT, 1, 2)
    skip_w = mm(vec[...], spread_m, NN, 3)[2:3]
    ssd[...] = ssd[...] + outside[...] + skip_w * x_all
    act = gat[...] * jax.nn.sigmoid(gat[...])
    gated[...] = ssd[...] * act
    scaled = gnm[...] * ggain
    q1 = jnp.sum(gated[...] * gated[...], axis=-1, keepdims=True)
    q2 = jnp.sum(scaled * gated[...], axis=-1, keepdims=True)
    packed = jnp.where(lane == 0, q1, jnp.where(lane == 1, q2, 0.0))
    stat_s[...] = packed.T[0:8]
    stats = [one(1 + t, stat_s, stat_r.at[t], ways[t]) for t in range(groups - 1)]
    for copy in stats:
        copy.start()
    for at in range(4):
        extt[at] = ext[HALO - 3 + at : HALO - 3 + at + length, inner:].T
    wbct[...] = wbc[...].astype(F32).T.astype(BF16)
    wst[...] = jnp.zeros_like(wst)
    wst[0:share] = wbct[pl.ds(pl.multiple_of(g * share, share), share)]
    wst[share : share + 16] = wdtp[0:16]
    for copy in stats:
        copy.wait()
    total = stat_s[...]
    for t in range(groups - 1):
        total = total + stat_r[t]
    st[0:8] = total
    cols = st[...].T
    rstd = lax.rsqrt(cols[:, 0:1] / full_inner + EPSILON)
    mean_dot = cols[:, 1:2] / full_inner
    sig_g = jax.nn.sigmoid(gat[...])
    act = gat[...] * sig_g
    scaled = gnm[...] * ggain
    grad_gated = rstd * scaled - gated[...] * (rstd * rstd * rstd * mean_dot)
    gs[...] = grad_gated * act
    gf[...] = gx[...] * gs[...]
    s_in[1] = mm(gf[...].T, cm[...], NN, 2)
    behind = Scan(1)
    behind.start()
    behind.point(0, points)
    nout[...] = (gated[...] * rstd * ggain).astype(BF16)

    cut = inner // 2
    sides = (
        (nout, rpa.at[0], owna.at[0], s2a.at[0], r2a.at[0]),
        (ggz, rpa.at[1], owna.at[1], s2a.at[1], r2a.at[1]),
    ) + tuple(
        (
            gcx.at[:, cols], rpa.at[2, :, cols], owna.at[2, :, cols],
            s2a.at[2, :, :, cols], r2a.at[2, :, :, cols],
        )
        for cols in (pl.ds(0, cut), pl.ds(cut, cut))
    ) + ((sidev, rpd, ownd, s2d, r2d),)

    def rs_first(ph):
        return remote(sides[ph][0], sides[ph][1], send1.at[ph], recv1.at[ph], partner)

    def rs_second(ph, t):
        return remote(
            sides[ph][3].at[t], sides[ph][4].at[t], send2.at[ph, t], recv2.at[ph, t], zpeer(t)
        )

    def rows_at(t):
        return pl.ds(pl.multiple_of(((k + 1 + t) % pairs) * part, part), part)

    def rs_mid(ph):
        mine, got, total, out = sides[ph][:4]
        near, other = (c_t, c_p) if ph == 0 else (n_t, n_p)
        first = mm(near[j], mine[...], NN)
        rs_first(ph).wait()
        total[...] = first + mm(other[...], got[...], NN)

        def pass_on(t):
            out[t] = total[rows_at(t)].astype(BF16)
            rs_second(ph, t).start()

        loop(pairs - 1, pass_on)

    def rs_end(ph, target):
        target[...] = sides[ph][2][rows_at(pairs - 1)]

        def collect(t):
            rs_second(ph, t).wait()
            target[...] += sides[ph][4][t].astype(F32)

        loop(pairs - 1, collect)

    rs_first(0).start()
    pv[...] = mm(nout[...], wout[...], NN)
    my_half = pl.ds(pl.multiple_of((g % 2) * half, half), half)
    other_half = pl.ds(pl.multiple_of((1 - g % 2) * half, half), half)
    out_give = one(4, pv.at[other_half], pr, mate)
    out_give.start()
    sig_g = jax.nn.sigmoid(gat[...])
    slope_g = sig_g * (1.0 + gat[...] * (1.0 - sig_g))
    grad_gated = rstd * (gnm[...] * ggain) - gated[...] * (rstd * rstd * rstd * mean_dot)
    ggz[...] = (grad_gated * ssd[...] * slope_g).astype(BF16)
    gmin[5:6] = jnp.sum(gnm[...] * gated[...] * rstd, axis=0, keepdims=True)
    behind.point(1, points)
    rs_first(1).start()

    gxa[...] = skip_w * gs[...]
    gmin[14:15] = jnp.sum(gs[...] * xh[...].astype(F32), axis=0, keepdims=True)
    gsc[...] = jnp.zeros_like(gsc)
    gcum[...] = narrow(gs[...] * outside[...])

    def back_pair(q):
        cols = slice(q * LANES, (q + 1) * LANES)
        x_pair = xh[:, cols]
        g_pair = gs[:, cols]
        total = None
        for side in range(2):
            h = 2 * q + side
            own = jnp.where(low_lane if side == 0 else ~low_lane, g_pair, 0.0)
            own_hi, own_lo = split(own, 2)
            grad_w = mm(own_hi, x_pair, NT) + mm(own_lo, x_pair, NT)
            d_row = rows_t[1, h : h + 1, :]
            plain = grad_w * decay_of(h)
            gsc[...] += plain * d_row
            inner_w = plain * scores
            csq[h : h + 1, :] = jnp.sum(inner_w, axis=0, keepdims=True)
            gcum[...] += jnp.where(
                lane == h, jnp.sum(inner_w * d_row, axis=1, keepdims=True), 0.0
            )
            gap_t = rows_t[0, h : h + 1, :] - tk[0, :, h : h + 1]
            w_t = scores_t * jnp.exp(jnp.where(ci >= ri, gap_t, -jnp.inf)) * tk[1, :, h : h + 1]
            w_hi, w_lo = split(w_t, 2)
            term = mm(w_hi, own_hi, NN) + mm(w_hi, own_lo, NN) + mm(w_lo, own_hi, NN)
            total = term if total is None else total + term
        gxa[:, cols] += total

    back_pair(0)
    behind.point(2, points)
    back_pair(1)
    back_pair(2)
    behind.point(3, points)
    c_give.wait()
    rs_mid(0)
    out_give.wait()
    po[...] = pv[my_half] + pr[...]
    out_far = one(5, po, pr2, far)
    out_far.start()
    back_pair(3)
    gcp[...] = mm(gf[...], s_out[0], NN, 2, 2) + mm(gsc[...], bm[...], NN, 2)
    gbp = mm(gsc[...].T, cm[...], NN, 2)
    n_give.wait()
    rs_mid(1)
    behind.finish()

    gw = mm(bm[...], s_out[1], NT, 1, 2)
    gpx[0:length] = (gxa[...] + tx[...] * gw) * slx[...]
    down = one(6, gpx.at[pl.ds(0, 8)], gpx.at[pl.ds(length, 8)], {"seq": (me + peers - 1) % peers})

    @pl.when(me > 0)
    def _():
        down.start()

    @pl.when(me == peers - 1)
    def _():
        gpx[length : length + 8] = jnp.zeros((8, inner), F32)
        gpb[:, length:] = jnp.zeros((share, LANES), F32)

    gbp = gbp + mm(wxs[...], s_out[1], NN, 2, 2)
    gbct[0:states] = gbp.T
    gbct[states:] = gcp[...].T

    def share_of(owner):
        return pl.ds(pl.multiple_of(owner * share, share), share)

    bc_gives = [
        one(7 + t, gbct.at[share_of((g + 1 + t) % groups)], hb_r.at[t], ways[t])
        for t in range(groups - 1)
    ]
    for copy in bc_gives:
        copy.start()

    grad_tail = narrow(gw * xh[...].astype(F32))
    tail_part = grad_tail * tk[3]
    st[0:8] = csq[...]
    csq_t = st[...].T
    grad_cum = gcum[...] - csq_t * tk[1] - tail_part
    grad_delta = grad_tail * tk[2] + csq_t
    prod = mm(spread_m, s_out[1] * s_out[0], NN, 1, 3)
    per_head = jnp.sum(prod, axis=1, keepdims=True)
    eye_r = lax.broadcasted_iota(jnp.int32, (LANES, LANES), 0)
    eye_c = lax.broadcasted_iota(jnp.int32, (LANES, LANES), 1)
    state_dot = jnp.sum(jnp.where(eye_r == eye_c, per_head, 0.0), axis=0, keepdims=True)
    growth_last = tk[4, length - 1 : length]
    grad_last = state_dot * growth_last + jnp.sum(tail_part, axis=0, keepdims=True)
    tri_t = jnp.where(ci >= ri, 1.0, 0.0).astype(BF16)
    grad_log = mm(tri_t, grad_cum, NN, 1, 3) + grad_last
    rates = -jnp.exp(vec[1:2])
    grad_u = (grad_delta + grad_log * rates) * tk[5]
    gmin[6:7, 0:LANES] = jnp.sum(grad_u, axis=0, keepdims=True)
    gmin[6:7, LANES : 2 * LANES] = rates * jnp.sum(grad_log * tk[1], axis=0, keepdims=True)
    gmin[6:7, 2 * LANES : 3 * LANES] = narrow(gmin[8:16])[6:7]
    gmin[14:15] = jnp.zeros((1, inner), F32)
    sidet[share : share + 8] = grad_u.T[0:8]

    @pl.when(me < peers - 1)
    def _():
        down.wait_recv()

    grad_in = None
    for at in range(4):
        term = cxw_ref[at : at + 1] * gpx[3 - at : 3 - at + length]
        grad_in = term if grad_in is None else grad_in + term
    gcx[...] = grad_in.astype(BF16)
    rs_first(2).start()
    rs_first(3).start()

    for copy in bc_gives:
        copy.wait()
    gp = gbct[share_of(g)]
    for t in range(groups - 1):
        gp = gp + hb_r[t]
    gp = gp * slbt[share_of(g)]
    gpb[:, 0:length] = gp
    down_bc = one(
        10, gpb.at[:, pl.ds(0, LANES)], gpb.at[:, pl.ds(length, LANES)],
        {"seq": (me + peers - 1) % peers},
    )

    @pl.when(me > 0)
    def _():
        down_bc.start()

    hp[...] = mm(ggz[...], wz[...], NT) + mm(gcx[...], wx[...], NT)
    rs_mid(2)
    rs_mid(3)
    for at in range(4):
        gmin[at : at + 1] = jnp.sum(
            gpx[0:length] * ext[HALO - 3 + at : HALO - 3 + at + length, 0:inner],
            axis=0, keepdims=True,
        )
    gmin[4:5] = jnp.sum(gpx[0:length], axis=0, keepdims=True)
    lane_s = lax.broadcasted_iota(jnp.int32, (LANES, LANES), 1)[0:share]
    conv_cols = jnp.where(lane_s == 4, jnp.sum(gp, axis=1, keepdims=True), 0.0)
    for at in range(4):
        conv_cols = jnp.where(
            lane_s == at, jnp.sum(gp * extt[at, share_of(g)], axis=1, keepdims=True), conv_cols
        )
    conv_cols = jnp.concatenate([conv_cols, jnp.zeros((LANES - share, LANES), F32)], axis=0)
    gmin[9:14, 0:LANES] = conv_cols.T[0:5]

    @pl.when(me < peers - 1)
    def _():
        down_bc.wait_recv()

    ge = gpb[...]
    taps = cbwt[share_of(g)]
    total = None
    for at in range(4):
        moved = ge if at == 3 else pltpu.roll(ge, length + LANES - (3 - at), 1)
        term = taps[:, at : at + 1] * moved[:, 0:length]
        total = term if total is None else total + term
    sidet[0:share] = total
    sidev[...] = sidet[...].T.astype(BF16)
    rs_first(4).start()
    hp[...] += mm(sidev[...], wst[...], NN)
    hp_give = one(11, hp.at[other_half], hr, mate)
    hp_give.start()
    residual = hid[...].astype(F32)
    pre = jnp.sum(hp[...] * (residual * rstd_of(residual)), axis=0, keepdims=True)
    for at in range(width // inner):
        gmin[7 + at : 8 + at] = pre[:, at * inner : (at + 1) * inner]
    minor_first = remote(gmin, rm1, send_m.at[pairs], recv_m.at[pairs], partner)
    minor_first.start()
    rs_mid(4)

    out_far.wait()
    out_o[my_half] = (hid[my_half].astype(F32) + (po[...] + pr2[...])).astype(BF16)
    out_back = one(12, out_o.at[my_half], out_o.at[my_half], mate)
    out_back.start()

    hp_give.wait()
    hq[...] = (hp[my_half] + hr[...]).astype(BF16)
    hp_far = one(13, hq, hr2, far)
    hp_far.start()
    minor_first.wait()
    sm[...] = gmin[...] + rm1[...]

    def minor_second(t):
        return remote(sm, rm2.at[t], send_m.at[t], recv_m.at[t], zpeer(t))

    loop(pairs - 1, lambda t: minor_second(t).start())
    hp_far.wait()
    grad_normed_in = hq[...].astype(F32) + hr2[...].astype(F32)
    residual = hid[my_half].astype(F32)
    in_rstd = rstd_of(residual)
    scaled_in = grad_normed_in * gain
    gh_o[my_half] = (
        cot[my_half].astype(F32)
        + in_rstd * scaled_in
        - residual
        * (in_rstd * in_rstd * in_rstd)
        * jnp.mean(scaled_in * residual, axis=-1, keepdims=True)
    )
    gh_back = one(14, gh_o.at[my_half], gh_o.at[my_half], mate)
    gh_back.start()
    loop(pairs - 1, lambda t: minor_second(t).wait())

    def ordered(q, total):
        slot = (k - q + pairs - 1) % pairs
        value = jnp.where(slot == pairs - 1, sm[...], rm2[jnp.minimum(slot, pairs - 2)])
        return total + value

    smh[g] = lax.fori_loop(0, pairs, ordered, jnp.zeros(sm.shape, F32))
    minor_heads = [one(15 + t, smh.at[g], smh.at[g], ways[t]) for t in range(groups - 1)]
    for copy in minor_heads:
        copy.start()
    min_o[...] = smh[g]
    rs_end(4, accd)
    shr[g] = accd[...]
    shares = [one(18 + t, shr.at[g], shr.at[g], ways[t]) for t in range(groups - 1)]
    for copy in shares:
        copy.start()
    rs_end(0, owna.at[0, pl.ds(0, part)])
    gwo_o[...] = owna[0, 0:part].T
    rs_end(1, gzx_o.at[:, pl.ds(0, inner)])
    gdt_o[...] = accd[...].T[share : share + heads]
    for copy in minor_heads:
        copy.wait()
    pre_sum = smh[0]
    for q in range(1, groups):
        pre_sum = pre_sum + smh[q]
    for at in range(width // inner):
        pre_o[:, at * inner : (at + 1) * inner] = pre_sum[7 + at : 8 + at]
    for q in range(groups // 2):
        left = smh[2 * q, 8:16, 0:LANES]
        right = pltpu.roll(smh[2 * q + 1, 8:16, 0:LANES], share, 1)
        cb_o[:, q * LANES : (q + 1) * LANES] = jnp.where(lane[0:8] < share, left, right)
    rs_end(2, gzx_o.at[:, pl.ds(inner, cut)])
    rs_end(3, gzx_o.at[:, pl.ds(inner + cut, cut)])
    for copy in shares:
        copy.wait()
    for q in range(groups // 2):
        right = pltpu.roll(shr[2 * q + 1], share, 1)
        gbc_o[:, q * LANES : (q + 1) * LANES] = jnp.where(lane[0:part] < share, shr[2 * q], right)

    out_back.wait()
    gh_back.wait()
    ahead.drain()
    behind.drain()

    @pl.when(me < peers - 1)
    def _():
        up.wait_send()

    @pl.when(me > 0)
    def _():
        down.wait_send()
        down_bc.wait_send()


def finish_kernel(
    out_i, gh_i, gzx_i, gbc_i, gdt_i, min_i, pre_i, cb_i, gwo_i,
    out_o, gh_o, gpre_o, gzx_o, gbc_o, gdt_o, cxw_o, cxb_o, cbw_o, cbb_o, dtb_o, alog_o, dsk_o,
    ggain_o, gwo_o,
):
    for source, target in ((out_i, out_o), (gh_i, gh_o), (gbc_i, gbc_o), (gdt_i, gdt_o), (gwo_i, gwo_o)):
        target[...] = source[...]
    inner = ggain_o.shape[1]
    heads = dtb_o.shape[1]
    gzx_o[:, 0, :] = gzx_i[:, 0:inner]
    gzx_o[:, 1, :] = gzx_i[:, inner:]
    gpre_o[...] = pre_i[...]
    cxw_o[...] = min_i[0:4]
    cxb_o[...] = min_i[4:5]
    ggain_o[...] = min_i[5:6]
    dtb_o[...] = min_i[6:7, 0:heads]
    alog_o[...] = min_i[6:7, LANES : LANES + heads]
    dsk_o[...] = min_i[6:7, 2 * LANES : 2 * LANES + heads]
    cbw_o[...] = cb_i[1:5]
    cbb_o[...] = cb_i[5:6]


def on_device(
    hidden, cotangent, pre_gain, w_zx, w_bc, w_dt, conv_x_w, conv_x_b, conv_bc_w, conv_bc_b,
    dt_bias, a_log, d_skip, gate_gain, w_out,
):
    peers, groups = lax.axis_size("seq"), lax.axis_size("head")
    pairs = peers // 2
    length, width = hidden.shape[1:]
    heads = dt_bias.shape[0]
    inner = w_zx.shape[2]
    hs = inner // heads
    bc = w_bc.shape[1]
    states = bc // 2
    share = bc // groups
    part = width // peers
    half = length // 2
    hh = heads // 2

    def row(value):
        return value.reshape(1, -1)

    def f32(*shape):
        return VMEM(shape, F32)

    def b16(*shape):
        return VMEM(shape, BF16)

    shapes = (
        ((length, width), BF16), ((length, width), F32), ((part, 2 * inner), F32),
        ((part, bc), F32), ((heads, part), F32), ((16, inner), F32), ((1, width), F32),
        ((8, bc), F32), ((inner, part), F32),
    )
    scratch = [
        b16(length, width), b16(length, width), b16(width, inner), b16(width, inner),
        b16(width, bc), b16(inner, width), b16(LANES, width),
        b16(HALO, width), b16(HALO + length, width), f32(HALO + length, inner + bc), f32(8, LANES),
        f32(length, inner), f32(bc, length), f32(4, bc, length), f32(bc, LANES),
        b16(length, inner), b16(length, states), b16(length, states),
        f32(6, length, LANES), f32(2, heads, length),
        f32(length, inner), f32(length, inner), f32(length, inner), f32(length, inner),
        f32(length, inner), f32(length, inner), f32(length, inner), f32(length, inner),
        f32(length, inner), f32(length, inner), b16(length, inner), b16(length, inner),
        f32(length, inner), f32(length, length), f32(length, LANES), f32(heads, length),
        f32(LANES, length), f32(8, length), f32(groups - 1, 8, length),
        f32(length + 8, inner), f32(share, length + LANES), f32(bc, length),
        f32(groups - 1, share, length), f32(LANES, length), b16(bc, width), b16(LANES, width),
        b16(length, inner), f32(length, states),
        b16(2, width // 2, length), b16(2, width // 2, length),
        b16(width // 2, length), b16(width // 2, length), b16(length, LANES),
        f32(heads, LANES), f32(2, inner, states), f32(2, inner, states),
        f32(2, hh, hs, states), f32(2, heads, LANES), f32(2, hh, hs, states),
        f32(2, hh, hs, states), f32(2, hh, hs, states),
        b16(3, length, inner), b16(length, LANES),
        f32(3, width // 2, inner), f32(width // 2, LANES),
        b16(3, pairs - 1, part, inner), b16(pairs - 1, part, LANES),
        b16(3, pairs - 1, part, inner), b16(pairs - 1, part, LANES),
        f32(part, LANES), f32(groups, part, LANES),
        f32(length, width), f32(half, width), f32(half, width), f32(half, width),
        f32(length, width), f32(half, width), b16(half, width), b16(half, width),
        f32(16, inner), f32(16, inner), f32(16, inner), f32(pairs - 1, 16, inner),
        f32(groups, 16, inner),
        DMA((6,)), DMA((23,)), DMA((23,)), DMA((2, 4, hh)), DMA((2, 4, hh)),
        DMA((5,)), DMA((5,)), DMA((5, pairs)), DMA((5, pairs)),
        DMA((pairs + 1,)), DMA((pairs + 1,)),
    ]
    sums = pl.pallas_call(
        functools.partial(layer_kernel, peers, groups),
        out_shape=tuple(jax.ShapeDtypeStruct(*s) for s in shapes),
        in_specs=[ANYWHERE] * 5 + [IN_VMEM] * 10,
        out_specs=(IN_VMEM,) * len(shapes),
        scratch_shapes=scratch,
        compiler_params=pltpu.CompilerParams(
            collective_id=1, has_side_effects=True, vmem_limit_bytes=60 * 2**20
        ),
        cost_estimate=pl.CostEstimate(flops=5 * 10**9, bytes_accessed=10**7, transcendentals=0),
        name="layer",
    )(
        hidden[0], cotangent[0], w_zx.transpose(1, 0, 2), w_bc, w_out, w_dt.T, row(pre_gain),
        conv_x_w, row(conv_x_b), conv_bc_w, row(conv_bc_b), row(dt_bias), row(a_log), row(d_skip),
        row(gate_gain),
    )
    finals = (
        ((length, width), BF16), ((length, width), F32), ((1, width), F32),
        ((part, 2, inner), F32), ((part, bc), F32), ((heads, part), F32), ((4, inner), F32),
        ((1, inner), F32), ((4, bc), F32), ((1, bc), F32), ((1, heads), F32), ((1, heads), F32),
        ((1, heads), F32), ((1, inner), F32), ((inner, part), F32),
    )
    done = pl.pallas_call(
        finish_kernel,
        out_shape=tuple(jax.ShapeDtypeStruct(*s) for s in finals),
        in_specs=[IN_VMEM] * len(shapes),
        out_specs=(IN_VMEM,) * len(finals),
        cost_estimate=pl.CostEstimate(flops=0, bytes_accessed=5 * 10**6, transcendentals=0),
        name="finish",
    )(*sums)
    lines = (2, 7, 9, 10, 11, 12, 13)
    done = [value.reshape(-1) if i in lines else value for i, value in enumerate(done)]
    return (done[0][None], done[1][None], *done[2:5], done[5].T, *done[6:])


def solution(mesh):
    return jax.shard_map(
        on_device,
        mesh=mesh,
        in_specs=(
            P(None, "seq", None), P(None, "seq", None), P(), P(None, None, "head"), P(),
            P(None, "head"), P(None, "head"), P("head"), P(), P(), P("head"), P("head"), P("head"),
            P("head"), P("head", None),
        ),
        out_specs=(
            P(None, "seq", None), P(None, "seq", None), P(), P("seq", None, "head"),
            P("seq", None), P("seq", "head"), P(None, "head"), P("head"), P(), P(), P("head"),
            P("head"), P("head"), P("head"), P("head", "seq"),
        ),
        check_vma=False,
    )
```

```python
import functools

import jax
import jax.numpy as jnp
from jax import lax
from jax.experimental import pallas as pl
from jax.experimental.pallas import tpu as pltpu
from jax.sharding import PartitionSpec as P

MESH = pl.DeviceIdType.MESH
VMEM = pltpu.VMEM
DMA = pltpu.SemaphoreType.DMA
IN_VMEM = pl.BlockSpec(memory_space=pltpu.VMEM)
ANYWHERE = pl.BlockSpec(memory_space=pl.ANY)

EPSILON = 1e-05
HALO = 16
LANES = 128
BF16, F32 = jnp.bfloat16, jnp.float32
NN, NT = ((1,), (0,)), ((1,), (1,))


def split(value, parts):
    if value.dtype == BF16:
        return [value]
    terms = []
    for at in range(parts):
        terms.append(value.astype(BF16))
        if at < parts - 1:
            value = value - terms[-1].astype(F32)
    return terms


def mm(left, right, dims, left_parts=1, right_parts=1):
    total = None
    most = max(left_parts, right_parts)
    rights = split(right, right_parts)
    for i, a in enumerate(split(left, left_parts)):
        for k, b in enumerate(rights):
            if i + k < most:
                term = lax.dot_general(a, b, (dims, ((), ())), preferred_element_type=F32)
                total = term if total is None else total + term
    return total


def low(values):
    return values.astype(BF16).astype(F32)


def softplus(values):
    return jnp.maximum(values, 0.0) + jnp.log1p(jnp.exp(-jnp.abs(values)))


def layer_kernel(
    peers, groups,
    hid_h, cot_h, wzx_h, wbc_h, wout_h, wdt_ref, gain_ref, cxw_ref, cxb_ref, cbw_ref, cbb_ref,
    dtb_ref, alog_ref, dsk_ref, ggain_ref,
    out_o, gh_o, gzx_o, gbc_o, gdt_o, min_o, pre_o, cb_o, gwo_o,
    raw, hid, cot, wz, wx, wbc, wout, wdtp, hal, nx, ext, vec, slx, slbt, extt, cbwt, xh, bm, cm,
    tk, rows_t, tx, gx, wxs, outside, gat, gnm, ssd, gated, gs, gf, ggz, nout, gxa, gsc, gcum, csq,
    st, stat_s, stat_r, gpx, gpb, gbct, hb_r, sidet, wbct, wst, gcx, gcp,
    n_t, c_t, n_p, c_p, sidev, dec8, s_in, s_out, part_s, part_d, carry_in, carry_out, back_out,
    rpa, rpd, owna, ownd, s2a, s2d, r2a, r2d, accd, shr,
    pv, pr, po, pr2, hp, hr, hq, hr2, gmin, rm1, sm, rm2, smh,
    lsem, ss, rs, sc_s, sc_r, send1, recv1, send2, recv2, send_m, recv_m,
):
    me, g = lax.axis_index("seq"), lax.axis_index("head")
    pairs = peers // 2
    k, j = me // 2, me % 2
    length, width = hid.shape
    inner = xh.shape[1]
    heads = dec8.shape[0]
    hs = inner // heads
    states = bm.shape[1]
    hh = heads // 2
    part = width // peers
    half = length // 2
    share = wbc.shape[1] // groups
    full_inner = inner * groups
    partner = {"seq": me + 1 - 2 * j}
    diagonal = {"seq": (me + peers - 1 + 2 * j) % peers}
    ways = [{"head": (g + 1 + t) % groups} for t in range(groups - 1)]
    mate = {"head": g + 1 - 2 * (g % 2)}
    far = {"head": (g + 2) % groups}
    unroll = pairs <= 4
    steps = pairs.bit_length() - 1

    def loop(count, body):
        if unroll:
            for t in range(count):
                body(t)
        else:
            pl.loop(0, count)(body)

    def zpeer(t):
        return {"seq": 2 * ((k + 1 + t) % pairs) + j}

    def remote(source, target, here, there, to):
        return pltpu.make_async_remote_copy(
            src_ref=source, dst_ref=target, send_sem=here, recv_sem=there,
            device_id=to, device_id_type=MESH,
        )

    def one(at, source, target, to):
        return remote(source, target, ss.at[at], rs.at[at], to)

    loads = [
        pltpu.make_async_copy(source, target, lsem.at[i])
        for i, (source, target) in enumerate((
            (hid_h, hid), (cot_h, cot), (wout_h, wout), (wzx_h, raw), (wbc_h, wbc),
        ))
    ]
    for copy in loads:
        copy.start()

    barrier = pltpu.get_barrier_semaphore()

    def greet(to):
        pl.semaphore_signal(barrier, inc=1, device_id=to, device_id_type=MESH)

    greet(partner)
    greet(diagonal)
    loop(pairs - 1, lambda t: greet(zpeer(t)))
    for to in ways:
        greet(to)

    wdtp[...] = jnp.zeros_like(wdtp)
    wdtp[0:heads] = wdt_ref[...]
    vec[...] = jnp.zeros_like(vec)
    vec[0:1, 0:heads] = dtb_ref[...]
    vec[1:2, 0:heads] = alog_ref[...]
    vec[2:3, 0:heads] = dsk_ref[...]
    st[...] = jnp.zeros_like(st)
    st[0:4] = cbw_ref[...]
    cbwt[...] = st[...].T
    st[...] = jnp.zeros_like(st)
    gmin[...] = jnp.zeros_like(gmin)
    sidet[...] = jnp.zeros_like(sidet)
    gain = gain_ref[...]
    ggain = ggain_ref[...]
    er = lax.broadcasted_iota(jnp.int32, (LANES, inner), 0) * hs
    ec = lax.broadcasted_iota(jnp.int32, (LANES, inner), 1)
    spread_m = jnp.where((ec >= er) & (ec < er + hs), 1.0, 0.0).astype(BF16)
    tr = lax.broadcasted_iota(jnp.int32, (inner, LANES), 1) * hs
    tc = lax.broadcasted_iota(jnp.int32, (inner, LANES), 0)
    gather_m = jnp.where((tc >= tr) & (tc < tr + hs), 1.0, 0.0).astype(BF16)
    ri = lax.broadcasted_iota(jnp.int32, (length, length), 0)
    ci = lax.broadcasted_iota(jnp.int32, (length, length), 1)
    lane = lax.broadcasted_iota(jnp.int32, (length, LANES), 1)

    def wide(value):
        return mm(value, spread_m, NN, 3)

    def narrow(value):
        return mm(value, gather_m, NN, 3)

    def rstd_of(values):
        return lax.rsqrt(jnp.mean(values * values, axis=-1, keepdims=True) + EPSILON)

    def normed_of(values):
        residual = values.astype(F32)
        return (residual * rstd_of(residual) * gain).astype(BF16)

    loads[0].wait()
    pl.semaphore_wait(barrier, pairs + groups)
    up = one(0, hid.at[pl.ds(length - HALO, HALO)], hal, {"seq": (me + 1) % peers})

    @pl.when(me < peers - 1)
    def _():
        up.start()

    @pl.when(me == 0)
    def _():
        hal[...] = jnp.zeros_like(hal)

    def turned(values, target):
        value = values.astype(F32).T.astype(BF16)
        for owner in range(peers):
            at = sum((owner // 2 >> step & 1) << steps - 1 - step for step in range(steps)) * part
            target[owner % 2, at : at + part] = value[owner * part : (owner + 1) * part]

    nx[HALO:] = normed_of(hid[...])
    loads[1].wait()
    turned(cot[...], c_t)
    c_give = one(21, c_t.at[1 - j], c_p, partner)
    c_give.start()
    loads[3].wait()
    wx[...] = raw[:, 1, :]
    loads[4].wait()

    @pl.when(me > 0)
    def _():
        up.wait_recv()

    nx[0:HALO] = normed_of(hal[...])
    ext[:, 0:inner] = low(mm(nx[...], wx[...], NN))
    ext[:, inner:] = low(mm(nx[...], wbc[...], NN))
    dt_raw = mm(wdtp[...], nx[HALO:], NT).T
    z = dt_raw + vec[0:1]
    delta = softplus(z)
    rates = -jnp.exp(vec[1:2])
    tri = jnp.where(ri >= ci, 1.0, 0.0).astype(BF16)
    cum = mm(tri, delta * rates, NN, 1, 3)
    last = cum[length - 1 : length]
    tail_exp = jnp.exp(last - cum)
    tk[0] = cum
    tk[1] = delta
    tk[2] = tail_exp
    tk[3] = tail_exp * delta
    tk[4] = jnp.exp(cum)
    tk[5] = jax.nn.sigmoid(z)
    cum_t = cum.T
    rows_t[0] = cum_t[0:heads]
    rows_t[1] = delta.T[0:heads]
    dec8[...] = jnp.broadcast_to(jnp.exp(cum_t[0:heads, length - 1 : length]), dec8.shape)

    def conv(cols, weight, offset_b):
        total = offset_b + weight[0:1] * ext[HALO - 3 : HALO - 3 + length, cols]
        for at in range(1, 4):
            total = total + weight[at : at + 1] * ext[HALO - 3 + at : HALO - 3 + at + length, cols]
        return total

    pre_x = conv(slice(0, inner), cxw_ref[...], cxb_ref[...])
    sig_x = jax.nn.sigmoid(pre_x)
    xh[...] = (pre_x * sig_x).astype(BF16)
    slx[...] = sig_x * (1.0 + pre_x * (1.0 - sig_x))
    pre_bc = conv(slice(inner, inner + 2 * states), cbw_ref[...], cbb_ref[...])
    sig_bc = jax.nn.sigmoid(pre_bc)
    bc_post = pre_bc * sig_bc
    bm[...] = bc_post[:, :states].astype(BF16)
    cm[...] = bc_post[:, states:].astype(BF16)
    slbt[...] = (sig_bc * (1.0 + pre_bc * (1.0 - sig_bc))).T
    tx[...] = wide(tk[3])
    wxs[...] = tx[...] * xh[...].astype(F32)
    s_in[0] = mm(wxs[...].T, bm[...], NN, 2)

    pieces, rows = carry_in.shape[1:3]

    class Scan:
        def __init__(self, way):
            self.way = way
            self.place = peers - 1 - me if way else me
            self.k, self.j = self.place // 2, self.place % 2
            self.mine = [
                pl.ds(pl.multiple_of((self.j * pieces + c) * rows, rows), rows)
                for c in range(pieces)
            ]
            theirs = [
                pl.ds(pl.multiple_of(((1 - self.j) * pieces + c) * rows, rows), rows)
                for c in range(pieces)
            ]
            onto = {"seq": (me + peers + (-2 if way else 2)) % peers}

            def copy(kind, c, source, target, to):
                return remote(source, target, sc_s.at[way, kind, c], sc_r.at[way, kind, c], to)

            self.give = [
                copy(0, c, s_in.at[way, theirs[c]], part_s.at[way, c], partner) for c in range(pieces)
            ]
            self.give_d = copy(3, 0, dec8, part_d.at[way], partner)
            self.onward = [
                copy(1, c, carry_out.at[way, c], carry_in.at[way, c], onto) for c in range(pieces)
            ]
            self.back = [
                copy(2, c, back_out.at[way, c], s_out.at[way, self.mine[c]], partner)
                for c in range(pieces)
            ]

        def start(self):
            self.give_d.start()
            for copy in self.give:
                copy.start()

            @pl.when(self.k == 0)
            def _():
                carry_in[self.way] = jnp.zeros(carry_in.shape[1:], F32)

        def step(self):
            way = self.way
            early = self.j == 0
            self.give_d.wait()
            for c in range(pieces):
                self.give[c].wait()
                row = pl.ds(self.j * hh + c // (pieces // hh), 1)
                own_s, own_d = s_in[way, self.mine[c]], dec8[row]
                got_s, got_d = part_s[way, c], part_d[way, row]
                s0, s1 = jnp.where(early, own_s, got_s), jnp.where(early, got_s, own_s)
                d0, d1 = jnp.where(early, own_d, got_d), jnp.where(early, got_d, own_d)

                @pl.when(self.k > 0)
                def _():
                    self.onward[c].wait_recv()

                before = carry_in[way, c]
                middle = d0 * before + s0

                @pl.when(self.k < pairs - 1)
                def _():
                    carry_out[way, c] = d1 * middle + s1
                    self.onward[c].start()

                back_out[way, c] = jnp.where(early, middle, before)
                self.back[c].start()
                s_out[way, self.mine[c]] = jnp.where(early, before, middle)

        def point(self, i, points):
            @pl.when(self.k == i if i < points - 1 else self.k >= i)
            def _():
                self.step()

        def finish(self):
            for c in range(pieces):
                self.back[c].wait()

        def drain(self):
            @pl.when(self.k < pairs - 1)
            def _():
                for c in range(pieces):
                    self.onward[c].wait_send()

    points = 4
    ahead = Scan(0)
    ahead.start()

    scores = mm(cm[...], bm[...], NT)
    scores_t = mm(bm[...], cm[...], NT)
    low_lane = lane < hs

    def decay_of(h):
        gap = tk[0, :, h : h + 1] - rows_t[0, h : h + 1, :]
        return jnp.exp(jnp.where(ri >= ci, gap, -jnp.inf))

    def inside_pair(q):
        cols = slice(q * LANES, (q + 1) * LANES)
        x_pair = xh[:, cols].astype(F32)
        total = None
        for side in range(2):
            h = 2 * q + side
            own = jnp.where(low_lane if side == 0 else ~low_lane, x_pair, 0.0).astype(BF16)
            weights = scores * decay_of(h) * rows_t[1, h : h + 1, :]
            term = mm(weights, own, NN, 2)
            total = term if total is None else total + term
        ssd[:, cols] = total

    ahead.point(0, points)
    turned(nx[HALO:], n_t)
    n_give = one(22, n_t.at[1 - j], n_p, partner)
    n_give.start()
    wz[...] = raw[:, 0, :]
    gat[...] = mm(nx[HALO:], wz[...], NN)
    inside_pair(0)
    ahead.point(1, points)
    inside_pair(1)
    inside_pair(2)
    ahead.point(2, points)
    inside_pair(3)
    loads[2].wait()
    gnm[...] = mm(cot[...], wout[...], NT)

    ahead.point(3, points)
    ahead.finish()

    x_all = xh[...].astype(F32)
    gx[...] = wide(tk[4])
    outside[...] = gx[...] * mm(cm[...], s_out[0], NT, 1, 2)
    skip_w = mm(vec[...], spread_m, NN, 3)[2:3]
    ssd[...] = ssd[...] + outside[...] + skip_w * x_all
    act = gat[...] * jax.nn.sigmoid(gat[...])
    gated[...] = ssd[...] * act
    scaled = gnm[...] * ggain
    q1 = jnp.sum(gated[...] * gated[...], axis=-1, keepdims=True)
    q2 = jnp.sum(scaled * gated[...], axis=-1, keepdims=True)
    packed = jnp.where(lane == 0, q1, jnp.where(lane == 1, q2, 0.0))
    stat_s[...] = packed.T[0:8]
    stats = [one(1 + t, stat_s, stat_r.at[t], ways[t]) for t in range(groups - 1)]
    for copy in stats:
        copy.start()
    for at in range(4):
        extt[at] = ext[HALO - 3 + at : HALO - 3 + at + length, inner:].T
    wbct[...] = wbc[...].astype(F32).T.astype(BF16)
    wst[...] = jnp.zeros_like(wst)
    wst[0:share] = wbct[pl.ds(pl.multiple_of(g * share, share), share)]
    wst[share : share + 16] = wdtp[0:16]
    for copy in stats:
        copy.wait()
    total = stat_s[...]
    for t in range(groups - 1):
        total = total + stat_r[t]
    st[0:8] = total
    cols = st[...].T
    rstd = lax.rsqrt(cols[:, 0:1] / full_inner + EPSILON)
    mean_dot = cols[:, 1:2] / full_inner
    sig_g = jax.nn.sigmoid(gat[...])
    act = gat[...] * sig_g
    scaled = gnm[...] * ggain
    grad_gated = rstd * scaled - gated[...] * (rstd * rstd * rstd * mean_dot)
    gs[...] = grad_gated * act
    gf[...] = gx[...] * gs[...]
    s_in[1] = mm(gf[...].T, cm[...], NN, 2)
    behind = Scan(1)
    behind.start()
    behind.point(0, points)
    nout[...] = (gated[...] * rstd * ggain).astype(BF16)

    cut = inner // 2
    sides = (
        (nout, rpa.at[0], owna.at[0], s2a.at[0], r2a.at[0]),
        (ggz, rpa.at[1], owna.at[1], s2a.at[1], r2a.at[1]),
    ) + tuple(
        (
            gcx.at[:, cols], rpa.at[2, :, cols], owna.at[2, :, cols],
            s2a.at[2, :, cols], r2a.at[2, :, cols],
        )
        for cols in (pl.ds(0, cut), pl.ds(cut, cut))
    ) + ((sidev, rpd, ownd, s2d, r2d),)

    def rs_first(ph):
        return remote(sides[ph][0], sides[ph][1], send1.at[ph], recv1.at[ph], partner)

    kept, sent, bases, peers_z = [], [], [], []
    offset, base = 0, 0
    for step in range(steps):
        size = width // 2 >> step + 1
        bit = k // 2**step % 2
        kept.append(pl.ds(pl.multiple_of(offset + bit * size, size), size))
        sent.append(pl.ds(pl.multiple_of(offset + (1 - bit) * size, size), size))
        bases.append(pl.ds(base, size))
        peers_z.append({"seq": 2 * (k + 2**step * (1 - 2 * bit)) + j})
        offset, base = offset + bit * size, base + size

    def rs_second(ph, step):
        return remote(
            sides[ph][3].at[sent[step]], sides[ph][4].at[bases[step]],
            send2.at[ph, step], recv2.at[ph, step], peers_z[step],
        )

    def rs_pass(ph, step):
        sides[ph][3][sent[step]] = sides[ph][2][sent[step]].astype(BF16)
        rs_second(ph, step).start()

    def rs_join(ph, step):
        rs_second(ph, step).wait()
        sides[ph][2][kept[step]] += sides[ph][4][bases[step]].astype(F32)

    def rs_mid(ph):
        mine, got, total = sides[ph][:3]
        near, other = (c_t, c_p) if ph == 0 else (n_t, n_p)
        first = mm(near[j], mine[...], NN)
        rs_first(ph).wait()
        total[...] = first + mm(other[...], got[...], NN)
        rs_pass(ph, 0)

    def rs_hop(ph):
        for step in range(1, steps):
            rs_join(ph, step - 1)
            rs_pass(ph, step)

    def rs_end(ph, target):
        rs_join(ph, steps - 1)
        target[...] = sides[ph][2][kept[-1]]

    rs_first(0).start()
    pv[...] = mm(nout[...], wout[...], NN)
    my_half = pl.ds(pl.multiple_of((g % 2) * half, half), half)
    other_half = pl.ds(pl.multiple_of((1 - g % 2) * half, half), half)
    out_give = one(4, pv.at[other_half], pr, mate)
    out_give.start()
    sig_g = jax.nn.sigmoid(gat[...])
    slope_g = sig_g * (1.0 + gat[...] * (1.0 - sig_g))
    grad_gated = rstd * (gnm[...] * ggain) - gated[...] * (rstd * rstd * rstd * mean_dot)
    ggz[...] = (grad_gated * ssd[...] * slope_g).astype(BF16)
    gmin[5:6] = jnp.sum(gnm[...] * gated[...] * rstd, axis=0, keepdims=True)
    behind.point(1, points)
    rs_first(1).start()

    gxa[...] = skip_w * gs[...]
    gmin[14:15] = jnp.sum(gs[...] * xh[...].astype(F32), axis=0, keepdims=True)
    gsc[...] = jnp.zeros_like(gsc)
    gcum[...] = narrow(gs[...] * outside[...])

    def back_pair(q):
        cols = slice(q * LANES, (q + 1) * LANES)
        x_pair = xh[:, cols]
        g_pair = gs[:, cols]
        total = None
        for side in range(2):
            h = 2 * q + side
            own = jnp.where(low_lane if side == 0 else ~low_lane, g_pair, 0.0)
            own_hi, own_lo = split(own, 2)
            grad_w = mm(own_hi, x_pair, NT) + mm(own_lo, x_pair, NT)
            d_row = rows_t[1, h : h + 1, :]
            plain = grad_w * decay_of(h)
            gsc[...] += plain * d_row
            inner_w = plain * scores
            csq[h : h + 1, :] = jnp.sum(inner_w, axis=0, keepdims=True)
            gcum[...] += jnp.where(
                lane == h, jnp.sum(inner_w * d_row, axis=1, keepdims=True), 0.0
            )
            gap_t = rows_t[0, h : h + 1, :] - tk[0, :, h : h + 1]
            w_t = scores_t * jnp.exp(jnp.where(ci >= ri, gap_t, -jnp.inf)) * tk[1, :, h : h + 1]
            w_hi, w_lo = split(w_t, 2)
            term = mm(w_hi, own_hi, NN) + mm(w_hi, own_lo, NN) + mm(w_lo, own_hi, NN)
            total = term if total is None else total + term
        gxa[:, cols] += total

    back_pair(0)
    out_give.wait()
    po[...] = pv[my_half] + pr[...]
    out_far = one(5, po, pr2, far)
    out_far.start()
    behind.point(2, points)
    back_pair(1)
    back_pair(2)
    behind.point(3, points)
    c_give.wait()
    rs_mid(0)
    back_pair(3)
    gcp[...] = mm(gf[...], s_out[0], NN, 2, 2) + mm(gsc[...], bm[...], NN, 2)
    gbp = mm(gsc[...].T, cm[...], NN, 2)
    n_give.wait()
    rs_mid(1)
    behind.finish()

    gw = mm(bm[...], s_out[1], NT, 1, 2)
    gpx[0:length] = (gxa[...] + tx[...] * gw) * slx[...]
    down = one(6, gpx.at[pl.ds(0, 8)], gpx.at[pl.ds(length, 8)], {"seq": (me + peers - 1) % peers})

    @pl.when(me > 0)
    def _():
        down.start()

    @pl.when(me == peers - 1)
    def _():
        gpx[length : length + 8] = jnp.zeros((8, inner), F32)
        gpb[:, length:] = jnp.zeros((share, LANES), F32)

    gbp = gbp + mm(wxs[...], s_out[1], NN, 2, 2)
    gbct[0:states] = gbp.T
    gbct[states:] = gcp[...].T

    def share_of(owner):
        return pl.ds(pl.multiple_of(owner * share, share), share)

    bc_gives = [
        one(7 + t, gbct.at[share_of((g + 1 + t) % groups)], hb_r.at[t], ways[t])
        for t in range(groups - 1)
    ]
    for copy in bc_gives:
        copy.start()
    rs_hop(0)

    grad_tail = narrow(gw * xh[...].astype(F32))
    tail_part = grad_tail * tk[3]
    st[0:8] = csq[...]
    csq_t = st[...].T
    grad_cum = gcum[...] - csq_t * tk[1] - tail_part
    grad_delta = grad_tail * tk[2] + csq_t
    prod = mm(spread_m, s_out[1] * s_out[0], NN, 1, 3)
    per_head = jnp.sum(prod, axis=1, keepdims=True)
    eye_r = lax.broadcasted_iota(jnp.int32, (LANES, LANES), 0)
    eye_c = lax.broadcasted_iota(jnp.int32, (LANES, LANES), 1)
    state_dot = jnp.sum(jnp.where(eye_r == eye_c, per_head, 0.0), axis=0, keepdims=True)
    growth_last = tk[4, length - 1 : length]
    grad_last = state_dot * growth_last + jnp.sum(tail_part, axis=0, keepdims=True)
    tri_t = jnp.where(ci >= ri, 1.0, 0.0).astype(BF16)
    grad_log = mm(tri_t, grad_cum, NN, 1, 3) + grad_last
    rates = -jnp.exp(vec[1:2])
    grad_u = (grad_delta + grad_log * rates) * tk[5]
    gmin[6:7, 0:LANES] = jnp.sum(grad_u, axis=0, keepdims=True)
    gmin[6:7, LANES : 2 * LANES] = rates * jnp.sum(grad_log * tk[1], axis=0, keepdims=True)
    gmin[6:7, 2 * LANES : 3 * LANES] = narrow(gmin[8:16])[6:7]
    gmin[14:15] = jnp.zeros((1, inner), F32)
    sidet[share : share + 8] = grad_u.T[0:8]

    @pl.when(me < peers - 1)
    def _():
        down.wait_recv()

    grad_in = None
    for at in range(4):
        term = cxw_ref[at : at + 1] * gpx[3 - at : 3 - at + length]
        grad_in = term if grad_in is None else grad_in + term
    gcx[...] = grad_in.astype(BF16)
    rs_first(2).start()
    rs_first(3).start()

    for copy in bc_gives:
        copy.wait()
    gp = gbct[share_of(g)]
    for t in range(groups - 1):
        gp = gp + hb_r[t]
    gp = gp * slbt[share_of(g)]
    gpb[:, 0:length] = gp
    down_bc = one(
        10, gpb.at[:, pl.ds(0, LANES)], gpb.at[:, pl.ds(length, LANES)],
        {"seq": (me + peers - 1) % peers},
    )

    @pl.when(me > 0)
    def _():
        down_bc.start()

    hp[...] = mm(ggz[...], wz[...], NT) + mm(gcx[...], wx[...], NT)
    for at in range(4):
        gmin[at : at + 1] = jnp.sum(
            gpx[0:length] * ext[HALO - 3 + at : HALO - 3 + at + length, 0:inner],
            axis=0, keepdims=True,
        )
    gmin[4:5] = jnp.sum(gpx[0:length], axis=0, keepdims=True)
    lane_s = lax.broadcasted_iota(jnp.int32, (LANES, LANES), 1)[0:share]
    conv_cols = jnp.where(lane_s == 4, jnp.sum(gp, axis=1, keepdims=True), 0.0)
    for at in range(4):
        conv_cols = jnp.where(
            lane_s == at, jnp.sum(gp * extt[at, share_of(g)], axis=1, keepdims=True), conv_cols
        )
    conv_cols = jnp.concatenate([conv_cols, jnp.zeros((LANES - share, LANES), F32)], axis=0)
    gmin[9:14, 0:LANES] = conv_cols.T[0:5]

    @pl.when(me < peers - 1)
    def _():
        down_bc.wait_recv()

    ge = gpb[...]
    taps = cbwt[share_of(g)]
    total = None
    for at in range(4):
        moved = ge if at == 3 else pltpu.roll(ge, length + LANES - (3 - at), 1)
        term = taps[:, at : at + 1] * moved[:, 0:length]
        total = term if total is None else total + term
    sidet[0:share] = total
    sidev[...] = sidet[...].T.astype(BF16)
    rs_first(4).start()
    hp[...] += mm(sidev[...], wst[...], NN)
    hp_give = one(11, hp.at[other_half], hr, mate)
    hp_give.start()
    residual = hid[...].astype(F32)
    pre = jnp.sum(hp[...] * (residual * rstd_of(residual)), axis=0, keepdims=True)
    for at in range(width // inner):
        gmin[7 + at : 8 + at] = pre[:, at * inner : (at + 1) * inner]
    minor_first = remote(gmin, rm1, send_m.at[pairs], recv_m.at[pairs], partner)
    minor_first.start()
    rs_mid(2)
    rs_mid(3)
    rs_hop(1)

    out_far.wait()
    out_o[my_half] = (hid[my_half].astype(F32) + (po[...] + pr2[...])).astype(BF16)
    out_back = one(12, out_o.at[my_half], out_o.at[my_half], mate)
    out_back.start()

    hp_give.wait()
    hq[...] = (hp[my_half] + hr[...]).astype(BF16)
    hp_far = one(13, hq, hr2, far)
    hp_far.start()
    rs_mid(4)
    minor_first.wait()
    sm[...] = gmin[...] + rm1[...]

    def minor_second(t):
        return remote(sm, rm2.at[t], send_m.at[t], recv_m.at[t], zpeer(t))

    loop(pairs - 1, lambda t: minor_second(t).start())
    rs_hop(2)
    rs_hop(3)
    hp_far.wait()
    grad_normed_in = hq[...].astype(F32) + hr2[...].astype(F32)
    residual = hid[my_half].astype(F32)
    in_rstd = rstd_of(residual)
    scaled_in = grad_normed_in * gain
    gh_o[my_half] = (
        cot[my_half].astype(F32)
        + in_rstd * scaled_in
        - residual
        * (in_rstd * in_rstd * in_rstd)
        * jnp.mean(scaled_in * residual, axis=-1, keepdims=True)
    )
    gh_back = one(14, gh_o.at[my_half], gh_o.at[my_half], mate)
    gh_back.start()
    rs_hop(4)
    loop(pairs - 1, lambda t: minor_second(t).wait())

    def ordered(q, total):
        slot = (k - q + pairs - 1) % pairs
        value = jnp.where(slot == pairs - 1, sm[...], rm2[jnp.minimum(slot, pairs - 2)])
        return total + value

    smh[g] = lax.fori_loop(0, pairs, ordered, jnp.zeros(sm.shape, F32))
    minor_heads = [one(15 + t, smh.at[g], smh.at[g], ways[t]) for t in range(groups - 1)]
    for copy in minor_heads:
        copy.start()
    min_o[...] = smh[g]
    rs_end(4, accd)
    shr[g] = accd[...]
    shares = [one(18 + t, shr.at[g], shr.at[g], ways[t]) for t in range(groups - 1)]
    for copy in shares:
        copy.start()
    rs_end(0, owna.at[0, pl.ds(0, part)])
    gwo_o[...] = owna[0, 0:part].T
    rs_end(1, gzx_o.at[:, pl.ds(0, inner)])
    gdt_o[...] = accd[...].T[share : share + heads]
    for copy in minor_heads:
        copy.wait()
    pre_sum = smh[0]
    for q in range(1, groups):
        pre_sum = pre_sum + smh[q]
    for at in range(width // inner):
        pre_o[:, at * inner : (at + 1) * inner] = pre_sum[7 + at : 8 + at]
    for q in range(groups // 2):
        left = smh[2 * q, 8:16, 0:LANES]
        right = pltpu.roll(smh[2 * q + 1, 8:16, 0:LANES], share, 1)
        cb_o[:, q * LANES : (q + 1) * LANES] = jnp.where(lane[0:8] < share, left, right)
    rs_end(2, gzx_o.at[:, pl.ds(inner, cut)])
    rs_end(3, gzx_o.at[:, pl.ds(inner + cut, cut)])
    for copy in shares:
        copy.wait()
    for q in range(groups // 2):
        right = pltpu.roll(shr[2 * q + 1], share, 1)
        gbc_o[:, q * LANES : (q + 1) * LANES] = jnp.where(lane[0:part] < share, shr[2 * q], right)

    out_back.wait()
    gh_back.wait()
    ahead.drain()
    behind.drain()

    @pl.when(me < peers - 1)
    def _():
        up.wait_send()

    @pl.when(me > 0)
    def _():
        down.wait_send()
        down_bc.wait_send()


def finish_kernel(
    out_i, gh_i, gzx_i, gbc_i, gdt_i, min_i, pre_i, cb_i, gwo_i,
    out_o, gh_o, gpre_o, gzx_o, gbc_o, gdt_o, cxw_o, cxb_o, cbw_o, cbb_o, dtb_o, alog_o, dsk_o,
    ggain_o, gwo_o,
):
    for source, target in ((out_i, out_o), (gh_i, gh_o), (gbc_i, gbc_o), (gdt_i, gdt_o), (gwo_i, gwo_o)):
        target[...] = source[...]
    inner = ggain_o.shape[1]
    heads = dtb_o.shape[1]
    gzx_o[:, 0, :] = gzx_i[:, 0:inner]
    gzx_o[:, 1, :] = gzx_i[:, inner:]
    gpre_o[...] = pre_i[...]
    cxw_o[...] = min_i[0:4]
    cxb_o[...] = min_i[4:5]
    ggain_o[...] = min_i[5:6]
    dtb_o[...] = min_i[6:7, 0:heads]
    alog_o[...] = min_i[6:7, LANES : LANES + heads]
    dsk_o[...] = min_i[6:7, 2 * LANES : 2 * LANES + heads]
    cbw_o[...] = cb_i[1:5]
    cbb_o[...] = cb_i[5:6]


def on_device(
    hidden, cotangent, pre_gain, w_zx, w_bc, w_dt, conv_x_w, conv_x_b, conv_bc_w, conv_bc_b,
    dt_bias, a_log, d_skip, gate_gain, w_out,
):
    peers, groups = lax.axis_size("seq"), lax.axis_size("head")
    pairs = peers // 2
    length, width = hidden.shape[1:]
    heads = dt_bias.shape[0]
    inner = w_zx.shape[2]
    hs = inner // heads
    bc = w_bc.shape[1]
    states = bc // 2
    share = bc // groups
    part = width // peers
    half = length // 2
    hh = heads // 2
    steps = pairs.bit_length() - 1
    piece = (2, 2 * hh, hs // 2, states)

    def row(value):
        return value.reshape(1, -1)

    def f32(*shape):
        return VMEM(shape, F32)

    def b16(*shape):
        return VMEM(shape, BF16)

    shapes = (
        ((length, width), BF16), ((length, width), F32), ((part, 2 * inner), F32),
        ((part, bc), F32), ((heads, part), F32), ((16, inner), F32), ((1, width), F32),
        ((8, bc), F32), ((inner, part), F32),
    )
    scratch = [
        b16(width, 2, inner),
        b16(length, width), b16(length, width), b16(width, inner), b16(width, inner),
        b16(width, bc), b16(inner, width), b16(LANES, width),
        b16(HALO, width), b16(HALO + length, width), f32(HALO + length, inner + bc), f32(8, LANES),
        f32(length, inner), f32(bc, length), f32(4, bc, length), f32(bc, LANES),
        b16(length, inner), b16(length, states), b16(length, states),
        f32(6, length, LANES), f32(2, heads, length),
        f32(length, inner), f32(length, inner), f32(length, inner), f32(length, inner),
        f32(length, inner), f32(length, inner), f32(length, inner), f32(length, inner),
        f32(length, inner), f32(length, inner), b16(length, inner), b16(length, inner),
        f32(length, inner), f32(length, length), f32(length, LANES), f32(heads, length),
        f32(LANES, length), f32(8, length), f32(groups - 1, 8, length),
        f32(length + 8, inner), f32(share, length + LANES), f32(bc, length),
        f32(groups - 1, share, length), f32(LANES, length), b16(bc, width), b16(LANES, width),
        b16(length, inner), f32(length, states),
        b16(2, width // 2, length), b16(2, width // 2, length),
        b16(width // 2, length), b16(width // 2, length), b16(length, LANES),
        f32(heads, LANES), f32(2, inner, states), f32(2, inner, states),
        f32(*piece), f32(2, heads, LANES), f32(*piece), f32(*piece), f32(*piece),
        b16(3, length, inner), b16(length, LANES),
        f32(3, width // 2, inner), f32(width // 2, LANES),
        b16(3, width // 2, inner), b16(width // 2, LANES),
        b16(3, width // 2, inner), b16(width // 2, LANES),
        f32(part, LANES), f32(groups, part, LANES),
        f32(length, width), f32(half, width), f32(half, width), f32(half, width),
        f32(length, width), f32(half, width), b16(half, width), b16(half, width),
        f32(16, inner), f32(16, inner), f32(16, inner), f32(pairs - 1, 16, inner),
        f32(groups, 16, inner),
        DMA((5,)), DMA((23,)), DMA((23,)), DMA((2, 4, piece[1])), DMA((2, 4, piece[1])),
        DMA((5,)), DMA((5,)), DMA((5, steps)), DMA((5, steps)),
        DMA((pairs + 1,)), DMA((pairs + 1,)),
    ]
    sums = pl.pallas_call(
        functools.partial(layer_kernel, peers, groups),
        out_shape=tuple(jax.ShapeDtypeStruct(*s) for s in shapes),
        in_specs=[ANYWHERE] * 5 + [IN_VMEM] * 10,
        out_specs=(IN_VMEM,) * len(shapes),
        scratch_shapes=scratch,
        compiler_params=pltpu.CompilerParams(
            collective_id=1, has_side_effects=True, vmem_limit_bytes=60 * 2**20
        ),
        cost_estimate=pl.CostEstimate(flops=5 * 10**9, bytes_accessed=10**7, transcendentals=0),
        name="layer",
    )(
        hidden[0], cotangent[0], w_zx, w_bc, w_out, w_dt.T, row(pre_gain),
        conv_x_w, row(conv_x_b), conv_bc_w, row(conv_bc_b), row(dt_bias), row(a_log), row(d_skip),
        row(gate_gain),
    )
    finals = (
        ((length, width), BF16), ((length, width), F32), ((1, width), F32),
        ((part, 2, inner), F32), ((part, bc), F32), ((heads, part), F32), ((4, inner), F32),
        ((1, inner), F32), ((4, bc), F32), ((1, bc), F32), ((1, heads), F32), ((1, heads), F32),
        ((1, heads), F32), ((1, inner), F32), ((inner, part), F32),
    )
    done = pl.pallas_call(
        finish_kernel,
        out_shape=tuple(jax.ShapeDtypeStruct(*s) for s in finals),
        in_specs=[IN_VMEM] * len(shapes),
        out_specs=(IN_VMEM,) * len(finals),
        cost_estimate=pl.CostEstimate(flops=0, bytes_accessed=5 * 10**6, transcendentals=0),
        name="finish",
    )(*sums)
    lines = (2, 7, 9, 10, 11, 12, 13)
    done = [value.reshape(-1) if i in lines else value for i, value in enumerate(done)]
    return (done[0][None], done[1][None], *done[2:5], done[5].T, *done[6:])


def solution(mesh):
    return jax.shard_map(
        on_device,
        mesh=mesh,
        in_specs=(
            P(None, "seq", None), P(None, "seq", None), P(), P(None, None, "head"), P(),
            P(None, "head"), P(None, "head"), P("head"), P(), P(), P("head"), P("head"), P("head"),
            P("head"), P("head", None),
        ),
        out_specs=(
            P(None, "seq", None), P(None, "seq", None), P(), P("seq", None, "head"),
            P("seq", None), P("seq", "head"), P(None, "head"), P("head"), P(), P(), P("head"),
            P("head"), P("head"), P("head"), P("head", "seq"),
        ),
        check_vma=False,
    )
```

```python
import functools

import jax
import jax.numpy as jnp
from jax import lax
from jax.experimental import pallas as pl
from jax.experimental.pallas import tpu as pltpu
from jax.sharding import PartitionSpec as P

MESH = pl.DeviceIdType.MESH
VMEM = pltpu.VMEM
DMA = pltpu.SemaphoreType.DMA
IN_VMEM = pl.BlockSpec(memory_space=pltpu.VMEM)
ANYWHERE = pl.BlockSpec(memory_space=pl.ANY)

EPSILON = 1e-05
HALO = 16
LANES = 128
BF16, F32 = jnp.bfloat16, jnp.float32
NN, NT = ((1,), (0,)), ((1,), (1,))


def split(value, parts):
    if value.dtype == BF16:
        return [value]
    terms = []
    for at in range(parts):
        terms.append(value.astype(BF16))
        if at < parts - 1:
            value = value - terms[-1].astype(F32)
    return terms


def mm(left, right, dims, left_parts=1, right_parts=1):
    total = None
    most = max(left_parts, right_parts)
    rights = split(right, right_parts)
    for i, a in enumerate(split(left, left_parts)):
        for k, b in enumerate(rights):
            if i + k < most:
                term = lax.dot_general(a, b, (dims, ((), ())), preferred_element_type=F32)
                total = term if total is None else total + term
    return total


def low(values):
    return values.astype(BF16).astype(F32)


def softplus(values):
    return jnp.maximum(values, 0.0) + jnp.log1p(jnp.exp(-jnp.abs(values)))


def layer_kernel(
    peers, groups,
    hid_h, cot_h, wzx_h, wbc_h, wout_h, wdt_ref, gain_ref, cxw_ref, cxb_ref, cbw_ref, cbb_ref,
    dtb_ref, alog_ref, dsk_ref, ggain_ref,
    out_o, gh_o, gzx_o, gbc_o, gdt_o, min_o, pre_o, cb_o, gwo_o,
    raw, hid, cot, wz, wx, wbc, wout, wdtp, hal, nx, ext, vec, slx, slbt, extt, cbwt, xh, bm, cm,
    tk, rows_t, tx, gx, wxs, outside, gat, gnm, ssd, gated, gs, gf, ggz, nout, gxa, gsc, gcum, csq,
    st, stat_s, stat_r, gpx, gpb, gbct, hb_r, sidet, wbct, wst, gcx, gcp,
    n_t, c_t, n_p, c_p, sidev, dec8, s_in, s_out, part_s, part_d, carry_in, carry_out, back_out,
    rpa, rpd, owna, ownd, s2a, s2d, r2a, r2d, accd, shr,
    pv, pr, po, pr2, hp, hr, hq, hr2, gmin, rm1, sm, rm2, smh,
    lsem, ss, rs, sc_s, sc_r, send1, recv1, send2, recv2, send_m, recv_m,
):
    me, g = lax.axis_index("seq"), lax.axis_index("head")
    pairs = peers // 2
    k, j = me // 2, me % 2
    length, width = hid.shape
    inner = xh.shape[1]
    heads = dec8.shape[0]
    hs = inner // heads
    states = bm.shape[1]
    hh = heads // 2
    part = width // peers
    half = length // 2
    share = wbc.shape[1] // groups
    full_inner = inner * groups
    partner = {"seq": me + 1 - 2 * j}
    diagonal = {"seq": (me + peers - 1 + 2 * j) % peers}
    ways = [{"head": (g + 1 + t) % groups} for t in range(groups - 1)]
    mate = {"head": g + 1 - 2 * (g % 2)}
    far = {"head": (g + 2) % groups}
    unroll = pairs <= 4
    steps = pairs.bit_length() - 1

    def loop(count, body):
        if unroll:
            for t in range(count):
                body(t)
        else:
            pl.loop(0, count)(body)

    def zpeer(t):
        return {"seq": 2 * ((k + 1 + t) % pairs) + j}

    def remote(source, target, here, there, to):
        return pltpu.make_async_remote_copy(
            src_ref=source, dst_ref=target, send_sem=here, recv_sem=there,
            device_id=to, device_id_type=MESH,
        )

    def one(at, source, target, to):
        return remote(source, target, ss.at[at], rs.at[at], to)

    loads = [
        pltpu.make_async_copy(source, target, lsem.at[i])
        for i, (source, target) in enumerate((
            (hid_h, hid), (cot_h, cot), (wout_h, wout), (wzx_h, raw), (wbc_h, wbc),
        ))
    ]
    for copy in loads:
        copy.start()

    barrier = pltpu.get_barrier_semaphore()

    def greet(to):
        pl.semaphore_signal(barrier, inc=1, device_id=to, device_id_type=MESH)

    greet(partner)
    greet(diagonal)
    loop(pairs - 1, lambda t: greet(zpeer(t)))
    for to in ways:
        greet(to)

    wdtp[...] = jnp.zeros_like(wdtp)
    wdtp[0:heads] = wdt_ref[...]
    vec[...] = jnp.zeros_like(vec)
    vec[0:1, 0:heads] = dtb_ref[...]
    vec[1:2, 0:heads] = alog_ref[...]
    vec[2:3, 0:heads] = dsk_ref[...]
    st[...] = jnp.zeros_like(st)
    st[0:4] = cbw_ref[...]
    cbwt[...] = st[...].T
    st[...] = jnp.zeros_like(st)
    gmin[...] = jnp.zeros_like(gmin)
    sidet[...] = jnp.zeros_like(sidet)
    gain = gain_ref[...]
    ggain = ggain_ref[...]
    er = lax.broadcasted_iota(jnp.int32, (LANES, inner), 0) * hs
    ec = lax.broadcasted_iota(jnp.int32, (LANES, inner), 1)
    spread_m = jnp.where((ec >= er) & (ec < er + hs), 1.0, 0.0).astype(BF16)
    tr = lax.broadcasted_iota(jnp.int32, (inner, LANES), 1) * hs
    tc = lax.broadcasted_iota(jnp.int32, (inner, LANES), 0)
    gather_m = jnp.where((tc >= tr) & (tc < tr + hs), 1.0, 0.0).astype(BF16)
    ri = lax.broadcasted_iota(jnp.int32, (length, length), 0)
    ci = lax.broadcasted_iota(jnp.int32, (length, length), 1)
    lane = lax.broadcasted_iota(jnp.int32, (length, LANES), 1)

    def wide(value):
        return mm(value, spread_m, NN, 3)

    def narrow(value):
        return mm(value, gather_m, NN, 3)

    def rstd_of(values):
        return lax.rsqrt(jnp.mean(values * values, axis=-1, keepdims=True) + EPSILON)

    def normed_of(values):
        residual = values.astype(F32)
        return (residual * rstd_of(residual) * gain).astype(BF16)

    loads[0].wait()
    pl.semaphore_wait(barrier, pairs + groups)
    up = one(0, hid.at[pl.ds(length - HALO, HALO)], hal, {"seq": (me + 1) % peers})

    @pl.when(me < peers - 1)
    def _():
        up.start()

    @pl.when(me == 0)
    def _():
        hal[...] = jnp.zeros_like(hal)

    def turned(values, target):
        value = values.astype(F32).T.astype(BF16)
        for owner in range(peers):
            at = sum((owner // 2 >> step & 1) << steps - 1 - step for step in range(steps)) * part
            target[owner % 2, at : at + part] = value[owner * part : (owner + 1) * part]

    nx[HALO:] = normed_of(hid[...])
    loads[1].wait()
    turned(cot[...], c_t)
    c_give = one(21, c_t.at[1 - j], c_p, partner)
    c_give.start()
    loads[3].wait()
    wx[...] = raw[:, 1, :]
    loads[4].wait()

    @pl.when(me > 0)
    def _():
        up.wait_recv()

    nx[0:HALO] = normed_of(hal[...])
    ext[:, 0:inner] = low(mm(nx[...], wx[...], NN))
    ext[:, inner:] = low(mm(nx[...], wbc[...], NN))
    dt_raw = mm(wdtp[...], nx[HALO:], NT).T
    z = dt_raw + vec[0:1]
    delta = softplus(z)
    rates = -jnp.exp(vec[1:2])
    tri = jnp.where(ri >= ci, 1.0, 0.0).astype(BF16)
    cum = mm(tri, delta * rates, NN, 1, 3)
    last = cum[length - 1 : length]
    tail_exp = jnp.exp(last - cum)
    tk[0] = cum
    tk[1] = delta
    tk[2] = tail_exp
    tk[3] = tail_exp * delta
    tk[4] = jnp.exp(cum)
    tk[5] = jax.nn.sigmoid(z)
    cum_t = cum.T
    rows_t[0] = cum_t[0:heads]
    rows_t[1] = delta.T[0:heads]
    dec8[...] = jnp.broadcast_to(jnp.exp(cum_t[0:heads, length - 1 : length]), dec8.shape)

    def conv(cols, weight, offset_b):
        total = offset_b + weight[0:1] * ext[HALO - 3 : HALO - 3 + length, cols]
        for at in range(1, 4):
            total = total + weight[at : at + 1] * ext[HALO - 3 + at : HALO - 3 + at + length, cols]
        return total

    pre_x = conv(slice(0, inner), cxw_ref[...], cxb_ref[...])
    sig_x = jax.nn.sigmoid(pre_x)
    xh[...] = (pre_x * sig_x).astype(BF16)
    slx[...] = sig_x * (1.0 + pre_x * (1.0 - sig_x))
    pre_bc = conv(slice(inner, inner + 2 * states), cbw_ref[...], cbb_ref[...])
    sig_bc = jax.nn.sigmoid(pre_bc)
    bc_post = pre_bc * sig_bc
    bm[...] = bc_post[:, :states].astype(BF16)
    cm[...] = bc_post[:, states:].astype(BF16)
    slbt[...] = (sig_bc * (1.0 + pre_bc * (1.0 - sig_bc))).T
    tx[...] = wide(tk[3])
    wxs[...] = tx[...] * xh[...].astype(F32)
    s_in[0] = mm(wxs[...].T, bm[...], NN, 2)

    pieces, rows = carry_in.shape[1:3]

    class Scan:
        def __init__(self, way):
            self.way = way
            self.place = peers - 1 - me if way else me
            self.k, self.j = self.place // 2, self.place % 2
            self.mine = [
                pl.ds(pl.multiple_of((self.j * pieces + c) * rows, rows), rows)
                for c in range(pieces)
            ]
            theirs = [
                pl.ds(pl.multiple_of(((1 - self.j) * pieces + c) * rows, rows), rows)
                for c in range(pieces)
            ]
            onto = {"seq": (me + peers + (-2 if way else 2)) % peers}

            def copy(kind, c, source, target, to):
                return remote(source, target, sc_s.at[way, kind, c], sc_r.at[way, kind, c], to)

            self.give = [
                copy(0, c, s_in.at[way, theirs[c]], part_s.at[way, c], partner) for c in range(pieces)
            ]
            self.give_d = copy(3, 0, dec8, part_d.at[way], partner)
            self.onward = [
                copy(1, c, carry_out.at[way, c], carry_in.at[way, c], onto) for c in range(pieces)
            ]
            self.back = [
                copy(2, c, back_out.at[way, c], s_out.at[way, self.mine[c]], partner)
                for c in range(pieces)
            ]

        def start(self):
            self.give_d.start()
            for copy in self.give:
                copy.start()

            @pl.when(self.k == 0)
            def _():
                carry_in[self.way] = jnp.zeros(carry_in.shape[1:], F32)

        def step(self):
            way = self.way
            early = self.j == 0
            self.give_d.wait()
            for c in range(pieces):
                self.give[c].wait()
                row = pl.ds(self.j * hh + c // (pieces // hh), 1)
                own_s, own_d = s_in[way, self.mine[c]], dec8[row]
                got_s, got_d = part_s[way, c], part_d[way, row]
                s0, s1 = jnp.where(early, own_s, got_s), jnp.where(early, got_s, own_s)
                d0, d1 = jnp.where(early, own_d, got_d), jnp.where(early, got_d, own_d)

                @pl.when(self.k > 0)
                def _():
                    self.onward[c].wait_recv()

                before = carry_in[way, c]
                middle = d0 * before + s0

                @pl.when(self.k < pairs - 1)
                def _():
                    carry_out[way, c] = d1 * middle + s1
                    self.onward[c].start()

                back_out[way, c] = jnp.where(early, middle, before)
                self.back[c].start()
                s_out[way, self.mine[c]] = jnp.where(early, before, middle)

        def point(self, i, points):
            @pl.when(self.k == i if i < points - 1 else self.k >= i)
            def _():
                self.step()

        def finish(self):
            for c in range(pieces):
                self.back[c].wait()

        def drain(self):
            @pl.when(self.k < pairs - 1)
            def _():
                for c in range(pieces):
                    self.onward[c].wait_send()

    points = 4
    ahead = Scan(0)
    ahead.start()

    scores = mm(cm[...], bm[...], NT)
    scores_t = mm(bm[...], cm[...], NT)
    low_lane = lane < hs

    def decay_of(h):
        gap = tk[0, :, h : h + 1] - rows_t[0, h : h + 1, :]
        return jnp.exp(jnp.where(ri >= ci, gap, -jnp.inf))

    def inside_pair(q):
        cols = slice(q * LANES, (q + 1) * LANES)
        x_pair = xh[:, cols].astype(F32)
        total = None
        for side in range(2):
            h = 2 * q + side
            own = jnp.where(low_lane if side == 0 else ~low_lane, x_pair, 0.0).astype(BF16)
            weights = scores * decay_of(h) * rows_t[1, h : h + 1, :]
            term = mm(weights, own, NN, 2)
            total = term if total is None else total + term
        ssd[:, cols] = total

    ahead.point(0, points)
    turned(nx[HALO:], n_t)
    n_give = one(22, n_t.at[1 - j], n_p, partner)
    n_give.start()
    wz[...] = raw[:, 0, :]
    gat[...] = mm(nx[HALO:], wz[...], NN)
    inside_pair(0)
    ahead.point(1, points)
    inside_pair(1)
    inside_pair(2)
    ahead.point(2, points)
    inside_pair(3)
    loads[2].wait()
    gnm[...] = mm(cot[...], wout[...], NT)

    ahead.point(3, points)
    ahead.finish()

    x_all = xh[...].astype(F32)
    gx[...] = wide(tk[4])
    outside[...] = gx[...] * mm(cm[...], s_out[0], NT, 1, 2)
    skip_w = mm(vec[...], spread_m, NN, 3)[2:3]
    ssd[...] = ssd[...] + outside[...] + skip_w * x_all
    act = gat[...] * jax.nn.sigmoid(gat[...])
    gated[...] = ssd[...] * act
    scaled = gnm[...] * ggain
    q1 = jnp.sum(gated[...] * gated[...], axis=-1, keepdims=True)
    q2 = jnp.sum(scaled * gated[...], axis=-1, keepdims=True)
    packed = jnp.where(lane == 0, q1, jnp.where(lane == 1, q2, 0.0))
    stat_s[...] = packed.T[0:8]
    stats = [one(1 + t, stat_s, stat_r.at[t], ways[t]) for t in range(groups - 1)]
    for copy in stats:
        copy.start()
    for at in range(4):
        extt[at] = ext[HALO - 3 + at : HALO - 3 + at + length, inner:].T
    wbct[...] = wbc[...].astype(F32).T.astype(BF16)
    wst[...] = jnp.zeros_like(wst)
    wst[0:share] = wbct[pl.ds(pl.multiple_of(g * share, share), share)]
    wst[share : share + 16] = wdtp[0:16]
    for copy in stats:
        copy.wait()
    total = stat_s[...]
    for t in range(groups - 1):
        total = total + stat_r[t]
    st[0:8] = total
    cols = st[...].T
    rstd = lax.rsqrt(cols[:, 0:1] / full_inner + EPSILON)
    mean_dot = cols[:, 1:2] / full_inner
    sig_g = jax.nn.sigmoid(gat[...])
    act = gat[...] * sig_g
    scaled = gnm[...] * ggain
    grad_gated = rstd * scaled - gated[...] * (rstd * rstd * rstd * mean_dot)
    gs[...] = grad_gated * act
    gf[...] = gx[...] * gs[...]
    s_in[1] = mm(gf[...].T, cm[...], NN, 2)
    behind = Scan(1)
    behind.start()
    behind.point(0, points)
    nout[...] = (gated[...] * rstd * ggain).astype(BF16)

    cut = inner // 2
    sides = (
        (nout, rpa.at[0], owna.at[0], s2a.at[0], r2a.at[0]),
        (ggz, rpa.at[1], owna.at[1], s2a.at[1], r2a.at[1]),
    ) + tuple(
        (
            gcx.at[:, cols], rpa.at[2, :, cols], owna.at[2, :, cols],
            s2a.at[2, :, cols], r2a.at[2, :, cols],
        )
        for cols in (pl.ds(0, cut), pl.ds(cut, cut))
    ) + ((sidev, rpd, ownd, s2d, r2d),)

    def rs_first(ph):
        return remote(sides[ph][0], sides[ph][1], send1.at[ph], recv1.at[ph], partner)

    kept, sent, bases, peers_z = [], [], [], []
    offset, base = 0, 0
    for step in range(steps):
        size = width // 2 >> step + 1
        bit = k // 2**step % 2
        kept.append(pl.ds(pl.multiple_of(offset + bit * size, size), size))
        sent.append(pl.ds(pl.multiple_of(offset + (1 - bit) * size, size), size))
        bases.append(pl.ds(base, size))
        peers_z.append({"seq": 2 * (k + 2**step * (1 - 2 * bit)) + j})
        offset, base = offset + bit * size, base + size

    def rs_second(ph, step):
        return remote(
            sides[ph][3].at[sent[step]], sides[ph][4].at[bases[step]],
            send2.at[ph, step], recv2.at[ph, step], peers_z[step],
        )

    def rs_pass(ph, step):
        sides[ph][3][sent[step]] = sides[ph][2][sent[step]].astype(BF16)
        rs_second(ph, step).start()

    def rs_join(ph, step):
        rs_second(ph, step).wait()
        sides[ph][2][kept[step]] += sides[ph][4][bases[step]].astype(F32)

    def rs_mid(ph):
        mine, got, total = sides[ph][:3]
        near, other = (c_t, c_p) if ph == 0 else (n_t, n_p)
        first = mm(near[j], mine[...], NN)
        rs_first(ph).wait()
        total[...] = first + mm(other[...], got[...], NN)
        rs_pass(ph, 0)

    def rs_hop(ph):
        for step in range(1, steps):
            rs_join(ph, step - 1)
            rs_pass(ph, step)

    def rs_end(ph, target):
        rs_join(ph, steps - 1)
        target[...] = sides[ph][2][kept[-1]]

    rs_first(0).start()
    pv[...] = mm(nout[...], wout[...], NN)
    my_half = pl.ds(pl.multiple_of((g % 2) * half, half), half)
    other_half = pl.ds(pl.multiple_of((1 - g % 2) * half, half), half)
    out_give = one(4, pv.at[other_half], pr, mate)
    out_give.start()
    sig_g = jax.nn.sigmoid(gat[...])
    slope_g = sig_g * (1.0 + gat[...] * (1.0 - sig_g))
    grad_gated = rstd * (gnm[...] * ggain) - gated[...] * (rstd * rstd * rstd * mean_dot)
    ggz[...] = (grad_gated * ssd[...] * slope_g).astype(BF16)
    gmin[5:6] = jnp.sum(gnm[...] * gated[...] * rstd, axis=0, keepdims=True)
    behind.point(1, points)
    rs_first(1).start()

    gxa[...] = skip_w * gs[...]
    gmin[14:15] = jnp.sum(gs[...] * xh[...].astype(F32), axis=0, keepdims=True)
    gsc[...] = jnp.zeros_like(gsc)
    gcum[...] = narrow(gs[...] * outside[...])

    def back_pair(q):
        cols = slice(q * LANES, (q + 1) * LANES)
        x_pair = xh[:, cols]
        g_pair = gs[:, cols]
        total = None
        for side in range(2):
            h = 2 * q + side
            own = jnp.where(low_lane if side == 0 else ~low_lane, g_pair, 0.0)
            own_hi, own_lo = split(own, 2)
            grad_w = mm(own_hi, x_pair, NT) + mm(own_lo, x_pair, NT)
            d_row = rows_t[1, h : h + 1, :]
            plain = grad_w * decay_of(h)
            gsc[...] += plain * d_row
            inner_w = plain * scores
            csq[h : h + 1, :] = jnp.sum(inner_w, axis=0, keepdims=True)
            gcum[...] += jnp.where(
                lane == h, jnp.sum(inner_w * d_row, axis=1, keepdims=True), 0.0
            )
            gap_t = rows_t[0, h : h + 1, :] - tk[0, :, h : h + 1]
            w_t = scores_t * jnp.exp(jnp.where(ci >= ri, gap_t, -jnp.inf)) * tk[1, :, h : h + 1]
            w_hi, w_lo = split(w_t, 2)
            term = mm(w_hi, own_hi, NN) + mm(w_hi, own_lo, NN) + mm(w_lo, own_hi, NN)
            total = term if total is None else total + term
        gxa[:, cols] += total

    back_pair(0)
    out_give.wait()
    po[...] = pv[my_half] + pr[...]
    out_far = one(5, po, pr2, far)
    out_far.start()
    behind.point(2, points)
    back_pair(1)
    back_pair(2)
    behind.point(3, points)
    c_give.wait()
    rs_mid(0)
    back_pair(3)
    gcp[...] = mm(gf[...], s_out[0], NN, 2, 2) + mm(gsc[...], bm[...], NN, 2)
    gbp = mm(gsc[...].T, cm[...], NN, 2)
    behind.finish()

    gw = mm(bm[...], s_out[1], NT, 1, 2)
    gpx[0:length] = (gxa[...] + tx[...] * gw) * slx[...]
    down = one(6, gpx.at[pl.ds(0, 8)], gpx.at[pl.ds(length, 8)], {"seq": (me + peers - 1) % peers})

    @pl.when(me > 0)
    def _():
        down.start()

    @pl.when(me == peers - 1)
    def _():
        gpx[length : length + 8] = jnp.zeros((8, inner), F32)
        gpb[:, length:] = jnp.zeros((share, LANES), F32)

    gbp = gbp + mm(wxs[...], s_out[1], NN, 2, 2)
    gbct[0:states] = gbp.T
    gbct[states:] = gcp[...].T

    def share_of(owner):
        return pl.ds(pl.multiple_of(owner * share, share), share)

    bc_gives = [
        one(7 + t, gbct.at[share_of((g + 1 + t) % groups)], hb_r.at[t], ways[t])
        for t in range(groups - 1)
    ]
    for copy in bc_gives:
        copy.start()

    grad_tail = narrow(gw * xh[...].astype(F32))
    tail_part = grad_tail * tk[3]
    st[0:8] = csq[...]
    csq_t = st[...].T
    grad_cum = gcum[...] - csq_t * tk[1] - tail_part
    grad_delta = grad_tail * tk[2] + csq_t
    prod = mm(spread_m, s_out[1] * s_out[0], NN, 1, 3)
    per_head = jnp.sum(prod, axis=1, keepdims=True)
    eye_r = lax.broadcasted_iota(jnp.int32, (LANES, LANES), 0)
    eye_c = lax.broadcasted_iota(jnp.int32, (LANES, LANES), 1)
    state_dot = jnp.sum(jnp.where(eye_r == eye_c, per_head, 0.0), axis=0, keepdims=True)
    growth_last = tk[4, length - 1 : length]
    grad_last = state_dot * growth_last + jnp.sum(tail_part, axis=0, keepdims=True)
    tri_t = jnp.where(ci >= ri, 1.0, 0.0).astype(BF16)
    grad_log = mm(tri_t, grad_cum, NN, 1, 3) + grad_last
    rates = -jnp.exp(vec[1:2])
    grad_u = (grad_delta + grad_log * rates) * tk[5]
    gmin[6:7, 0:LANES] = jnp.sum(grad_u, axis=0, keepdims=True)
    gmin[6:7, LANES : 2 * LANES] = rates * jnp.sum(grad_log * tk[1], axis=0, keepdims=True)
    gmin[6:7, 2 * LANES : 3 * LANES] = narrow(gmin[8:16])[6:7]
    gmin[14:15] = jnp.zeros((1, inner), F32)
    sidet[share : share + 8] = grad_u.T[0:8]

    @pl.when(me < peers - 1)
    def _():
        down.wait_recv()

    grad_in = None
    for at in range(4):
        term = cxw_ref[at : at + 1] * gpx[3 - at : 3 - at + length]
        grad_in = term if grad_in is None else grad_in + term
    gcx[...] = grad_in.astype(BF16)
    rs_first(2).start()
    rs_first(3).start()
    rs_hop(0)
    n_give.wait()
    rs_mid(1)

    for copy in bc_gives:
        copy.wait()
    gp = gbct[share_of(g)]
    for t in range(groups - 1):
        gp = gp + hb_r[t]
    gp = gp * slbt[share_of(g)]
    gpb[:, 0:length] = gp
    down_bc = one(
        10, gpb.at[:, pl.ds(0, LANES)], gpb.at[:, pl.ds(length, LANES)],
        {"seq": (me + peers - 1) % peers},
    )

    @pl.when(me > 0)
    def _():
        down_bc.start()

    hp[...] = mm(ggz[...], wz[...], NT) + mm(gcx[...], wx[...], NT)
    for at in range(4):
        gmin[at : at + 1] = jnp.sum(
            gpx[0:length] * ext[HALO - 3 + at : HALO - 3 + at + length, 0:inner],
            axis=0, keepdims=True,
        )
    gmin[4:5] = jnp.sum(gpx[0:length], axis=0, keepdims=True)
    lane_s = lax.broadcasted_iota(jnp.int32, (LANES, LANES), 1)[0:share]
    conv_cols = jnp.where(lane_s == 4, jnp.sum(gp, axis=1, keepdims=True), 0.0)
    for at in range(4):
        conv_cols = jnp.where(
            lane_s == at, jnp.sum(gp * extt[at, share_of(g)], axis=1, keepdims=True), conv_cols
        )
    conv_cols = jnp.concatenate([conv_cols, jnp.zeros((LANES - share, LANES), F32)], axis=0)
    gmin[9:14, 0:LANES] = conv_cols.T[0:5]

    @pl.when(me < peers - 1)
    def _():
        down_bc.wait_recv()

    ge = gpb[...]
    taps = cbwt[share_of(g)]
    total = None
    for at in range(4):
        moved = ge if at == 3 else pltpu.roll(ge, length + LANES - (3 - at), 1)
        term = taps[:, at : at + 1] * moved[:, 0:length]
        total = term if total is None else total + term
    sidet[0:share] = total
    sidev[...] = sidet[...].T.astype(BF16)
    rs_first(4).start()
    hp[...] += mm(sidev[...], wst[...], NN)
    hp_give = one(11, hp.at[other_half], hr, mate)
    hp_give.start()
    residual = hid[...].astype(F32)
    pre = jnp.sum(hp[...] * (residual * rstd_of(residual)), axis=0, keepdims=True)
    for at in range(width // inner):
        gmin[7 + at : 8 + at] = pre[:, at * inner : (at + 1) * inner]
    minor_first = remote(gmin, rm1, send_m.at[pairs], recv_m.at[pairs], partner)
    minor_first.start()
    rs_mid(2)
    rs_mid(3)
    rs_hop(1)

    out_far.wait()
    out_o[my_half] = (hid[my_half].astype(F32) + (po[...] + pr2[...])).astype(BF16)
    out_back = one(12, out_o.at[my_half], out_o.at[my_half], mate)
    out_back.start()

    hp_give.wait()
    hq[...] = (hp[my_half] + hr[...]).astype(BF16)
    hp_far = one(13, hq, hr2, far)
    hp_far.start()
    rs_mid(4)
    minor_first.wait()
    sm[...] = gmin[...] + rm1[...]

    def minor_second(t):
        return remote(sm, rm2.at[t], send_m.at[t], recv_m.at[t], zpeer(t))

    loop(pairs - 1, lambda t: minor_second(t).start())
    rs_hop(2)
    rs_hop(3)
    hp_far.wait()
    grad_normed_in = hq[...].astype(F32) + hr2[...].astype(F32)
    residual = hid[my_half].astype(F32)
    in_rstd = rstd_of(residual)
    scaled_in = grad_normed_in * gain
    gh_o[my_half] = (
        cot[my_half].astype(F32)
        + in_rstd * scaled_in
        - residual
        * (in_rstd * in_rstd * in_rstd)
        * jnp.mean(scaled_in * residual, axis=-1, keepdims=True)
    )
    gh_back = one(14, gh_o.at[my_half], gh_o.at[my_half], mate)
    gh_back.start()
    rs_hop(4)
    loop(pairs - 1, lambda t: minor_second(t).wait())

    def ordered(q, total):
        slot = (k - q + pairs - 1) % pairs
        value = jnp.where(slot == pairs - 1, sm[...], rm2[jnp.minimum(slot, pairs - 2)])
        return total + value

    smh[g] = lax.fori_loop(0, pairs, ordered, jnp.zeros(sm.shape, F32))
    minor_heads = [one(15 + t, smh.at[g], smh.at[g], ways[t]) for t in range(groups - 1)]
    for copy in minor_heads:
        copy.start()
    min_o[...] = smh[g]
    rs_end(4, accd)
    shr[g] = accd[...]
    shares = [one(18 + t, shr.at[g], shr.at[g], ways[t]) for t in range(groups - 1)]
    for copy in shares:
        copy.start()
    rs_end(0, owna.at[0, pl.ds(0, part)])
    gwo_o[...] = owna[0, 0:part].T
    rs_end(1, gzx_o.at[:, pl.ds(0, inner)])
    gdt_o[...] = accd[...].T[share : share + heads]
    for copy in minor_heads:
        copy.wait()
    pre_sum = smh[0]
    for q in range(1, groups):
        pre_sum = pre_sum + smh[q]
    for at in range(width // inner):
        pre_o[:, at * inner : (at + 1) * inner] = pre_sum[7 + at : 8 + at]
    for q in range(groups // 2):
        left = smh[2 * q, 8:16, 0:LANES]
        right = pltpu.roll(smh[2 * q + 1, 8:16, 0:LANES], share, 1)
        cb_o[:, q * LANES : (q + 1) * LANES] = jnp.where(lane[0:8] < share, left, right)
    rs_end(2, gzx_o.at[:, pl.ds(inner, cut)])
    rs_end(3, gzx_o.at[:, pl.ds(inner + cut, cut)])
    for copy in shares:
        copy.wait()
    for q in range(groups // 2):
        right = pltpu.roll(shr[2 * q + 1], share, 1)
        gbc_o[:, q * LANES : (q + 1) * LANES] = jnp.where(lane[0:part] < share, shr[2 * q], right)

    out_back.wait()
    gh_back.wait()
    ahead.drain()
    behind.drain()

    @pl.when(me < peers - 1)
    def _():
        up.wait_send()

    @pl.when(me > 0)
    def _():
        down.wait_send()
        down_bc.wait_send()


def finish_kernel(
    out_i, gh_i, gzx_i, gbc_i, gdt_i, min_i, pre_i, cb_i, gwo_i,
    out_o, gh_o, gpre_o, gzx_o, gbc_o, gdt_o, cxw_o, cxb_o, cbw_o, cbb_o, dtb_o, alog_o, dsk_o,
    ggain_o, gwo_o,
):
    for source, target in ((out_i, out_o), (gh_i, gh_o), (gbc_i, gbc_o), (gdt_i, gdt_o), (gwo_i, gwo_o)):
        target[...] = source[...]
    inner = ggain_o.shape[1]
    heads = dtb_o.shape[1]
    gzx_o[:, 0, :] = gzx_i[:, 0:inner]
    gzx_o[:, 1, :] = gzx_i[:, inner:]
    gpre_o[...] = pre_i[...]
    cxw_o[...] = min_i[0:4]
    cxb_o[...] = min_i[4:5]
    ggain_o[...] = min_i[5:6]
    dtb_o[...] = min_i[6:7, 0:heads]
    alog_o[...] = min_i[6:7, LANES : LANES + heads]
    dsk_o[...] = min_i[6:7, 2 * LANES : 2 * LANES + heads]
    cbw_o[...] = cb_i[1:5]
    cbb_o[...] = cb_i[5:6]


def on_device(
    hidden, cotangent, pre_gain, w_zx, w_bc, w_dt, conv_x_w, conv_x_b, conv_bc_w, conv_bc_b,
    dt_bias, a_log, d_skip, gate_gain, w_out,
):
    peers, groups = lax.axis_size("seq"), lax.axis_size("head")
    pairs = peers // 2
    length, width = hidden.shape[1:]
    heads = dt_bias.shape[0]
    inner = w_zx.shape[2]
    hs = inner // heads
    bc = w_bc.shape[1]
    states = bc // 2
    share = bc // groups
    part = width // peers
    half = length // 2
    hh = heads // 2
    steps = pairs.bit_length() - 1
    piece = (2, 2 * hh, hs // 2, states)

    def row(value):
        return value.reshape(1, -1)

    def f32(*shape):
        return VMEM(shape, F32)

    def b16(*shape):
        return VMEM(shape, BF16)

    shapes = (
        ((length, width), BF16), ((length, width), F32), ((part, 2 * inner), F32),
        ((part, bc), F32), ((heads, part), F32), ((16, inner), F32), ((1, width), F32),
        ((8, bc), F32), ((inner, part), F32),
    )
    scratch = [
        b16(width, 2, inner),
        b16(length, width), b16(length, width), b16(width, inner), b16(width, inner),
        b16(width, bc), b16(inner, width), b16(LANES, width),
        b16(HALO, width), b16(HALO + length, width), f32(HALO + length, inner + bc), f32(8, LANES),
        f32(length, inner), f32(bc, length), f32(4, bc, length), f32(bc, LANES),
        b16(length, inner), b16(length, states), b16(length, states),
        f32(6, length, LANES), f32(2, heads, length),
        f32(length, inner), f32(length, inner), f32(length, inner), f32(length, inner),
        f32(length, inner), f32(length, inner), f32(length, inner), f32(length, inner),
        f32(length, inner), f32(length, inner), b16(length, inner), b16(length, inner),
        f32(length, inner), f32(length, length), f32(length, LANES), f32(heads, length),
        f32(LANES, length), f32(8, length), f32(groups - 1, 8, length),
        f32(length + 8, inner), f32(share, length + LANES), f32(bc, length),
        f32(groups - 1, share, length), f32(LANES, length), b16(bc, width), b16(LANES, width),
        b16(length, inner), f32(length, states),
        b16(2, width // 2, length), b16(2, width // 2, length),
        b16(width // 2, length), b16(width // 2, length), b16(length, LANES),
        f32(heads, LANES), f32(2, inner, states), f32(2, inner, states),
        f32(*piece), f32(2, heads, LANES), f32(*piece), f32(*piece), f32(*piece),
        b16(3, length, inner), b16(length, LANES),
        f32(3, width // 2, inner), f32(width // 2, LANES),
        b16(3, width // 2, inner), b16(width // 2, LANES),
        b16(3, width // 2, inner), b16(width // 2, LANES),
        f32(part, LANES), f32(groups, part, LANES),
        f32(length, width), f32(half, width), f32(half, width), f32(half, width),
        f32(length, width), f32(half, width), b16(half, width), b16(half, width),
        f32(16, inner), f32(16, inner), f32(16, inner), f32(pairs - 1, 16, inner),
        f32(groups, 16, inner),
        DMA((5,)), DMA((23,)), DMA((23,)), DMA((2, 4, piece[1])), DMA((2, 4, piece[1])),
        DMA((5,)), DMA((5,)), DMA((5, steps)), DMA((5, steps)),
        DMA((pairs + 1,)), DMA((pairs + 1,)),
    ]
    sums = pl.pallas_call(
        functools.partial(layer_kernel, peers, groups),
        out_shape=tuple(jax.ShapeDtypeStruct(*s) for s in shapes),
        in_specs=[ANYWHERE] * 5 + [IN_VMEM] * 10,
        out_specs=(IN_VMEM,) * len(shapes),
        scratch_shapes=scratch,
        compiler_params=pltpu.CompilerParams(
            collective_id=1, has_side_effects=True, vmem_limit_bytes=60 * 2**20
        ),
        cost_estimate=pl.CostEstimate(flops=5 * 10**9, bytes_accessed=10**7, transcendentals=0),
        name="layer",
    )(
        hidden[0], cotangent[0], w_zx, w_bc, w_out, w_dt.T, row(pre_gain),
        conv_x_w, row(conv_x_b), conv_bc_w, row(conv_bc_b), row(dt_bias), row(a_log), row(d_skip),
        row(gate_gain),
    )
    finals = (
        ((length, width), BF16), ((length, width), F32), ((1, width), F32),
        ((part, 2, inner), F32), ((part, bc), F32), ((heads, part), F32), ((4, inner), F32),
        ((1, inner), F32), ((4, bc), F32), ((1, bc), F32), ((1, heads), F32), ((1, heads), F32),
        ((1, heads), F32), ((1, inner), F32), ((inner, part), F32),
    )
    done = pl.pallas_call(
        finish_kernel,
        out_shape=tuple(jax.ShapeDtypeStruct(*s) for s in finals),
        in_specs=[IN_VMEM] * len(shapes),
        out_specs=(IN_VMEM,) * len(finals),
        cost_estimate=pl.CostEstimate(flops=0, bytes_accessed=5 * 10**6, transcendentals=0),
        name="finish",
    )(*sums)
    lines = (2, 7, 9, 10, 11, 12, 13)
    done = [value.reshape(-1) if i in lines else value for i, value in enumerate(done)]
    return (done[0][None], done[1][None], *done[2:5], done[5].T, *done[6:])


def solution(mesh):
    return jax.shard_map(
        on_device,
        mesh=mesh,
        in_specs=(
            P(None, "seq", None), P(None, "seq", None), P(), P(None, None, "head"), P(),
            P(None, "head"), P(None, "head"), P("head"), P(), P(), P("head"), P("head"), P("head"),
            P("head"), P("head", None),
        ),
        out_specs=(
            P(None, "seq", None), P(None, "seq", None), P(), P("seq", None, "head"),
            P("seq", None), P("seq", "head"), P(None, "head"), P("head"), P(), P(), P("head"),
            P("head"), P("head"), P("head"), P("head", "seq"),
        ),
        check_vma=False,
    )
```
